128 devices in a mesh: prow: 8 (over y_lo, x), pcol: 16 (over y_hi, z, core).
Axes of the slice: x: 4, y: 4 (y_hi: 2, y_lo: 2; y = y_hi * 2 + y_lo), z: 4, core: 2. Of those that a mesh axis runs over, the one named last changes fastest.
Arguments:
- l_panel: bfloat16 [16384, 2048], P('prow', 'pcol'), may hold values from -0.29882812 to 0.29882812
- inverse_tile: bfloat16 [16384, 16384], P('prow', 'pcol'), may hold values from -0.375 to 0.375
- unit_inverse: bfloat16 [16, 128, 128], P('pcol'), may hold values from -0.5 to 0.5
- pivot_inverse: float32 [16, 128, 128], P('pcol'), may hold values from -6 to 6
- listed: int32 [16, 128], replicated, may hold values 0 or 1
Outputs:
- offdiag: float32 [2048, 16384], P('pcol', 'prow')
- diag: float32 [16, 128, 128], P('pcol')
The draws below stay inside these ranges and needn't reach their ends.
All inputs are finite; a program needn't handle non-finite values.
Results may differ from the reference program's by a relative error of at most 0.015.
Values may be sent and summed in bfloat16 or wider, within the bound.
A program may use at most 64 MiB of HBM per device.

```python
import jax
import jax.numpy as jnp
from jax import lax

W = 128
BLOCK = 128
S = 16
NBLK = 128
NA = 16384
N_PCOL = 16


def plant(values, key, least, top_value):
    longest = values.shape.index(max(values.shape))
    spots = []
    for shift in (0, 1):
        where = [jax.random.randint(jax.random.fold_in(key, axis), (), 0, length) for axis, length in enumerate(values.shape)]
        where[longest] = (where[longest] + shift) % values.shape[longest]
        spots.append(tuple(where))
    return values.at[spots[0]].set(least).at[spots[1]].set(top_value)


def block_levels(key, extent, shards, smallest, high):
    def one(axis_at, shards_of):
        draws = jax.random.uniform(jax.random.fold_in(jax.random.fold_in(key, 6), axis_at), (shards_of,), jnp.float32, smallest / len(shards), high / len(shards))
        return jnp.repeat(jnp.exp(draws), extent[axis_at] // shards_of).reshape((-1,) + (1,) * (len(extent) - axis_at - 1))

    loudness = one(*shards[0])
    for cut in shards[1:]:
        loudness = loudness * one(*cut)
    return loudness


def gaussian(stream_key, shape, deviation, bound, shards=(), held_as=jnp.bfloat16):
    values = deviation * jax.random.normal(stream_key, shape, jnp.float32)
    if shards:
        values = values * block_levels(stream_key, shape, shards, -0.22, 0.18)
    return jnp.clip(values, -bound, bound).astype(held_as)


def setup_inputs(seed: int = 0) -> dict:
    splits = jax.random.split(jax.random.key(seed), 6)
    l_panel = gaussian(splits[0], (NA, S * W), 0.05, 0.29882812, ((0, 8), (1, 16)))
    inverse_tile = gaussian(splits[1], (NA, NA), (NA // 64) ** -0.5, 0.375, ((0, 8), (1, 16)))
    unit_inverse = gaussian(splits[2], (S, W, W), W ** -0.5, 0.5, ((0, 16),))
    pivot_inverse = gaussian(splits[3], (S, W, W), 1.0, 6.0, ((0, 16),), jnp.float32)
    listed = plant((jax.random.randint(splits[4], (S, NBLK), 0, 4) < 3).astype(jnp.int32), jax.random.fold_in(splits[4], 1), 0, 1)
    return {"l_panel": l_panel, "inverse_tile": inverse_tile, "unit_inverse": unit_inverse, "pivot_inverse": pivot_inverse, "listed": listed}


def reference(l_panel, inverse_tile, unit_inverse, pivot_inverse, listed):
    row_mask = jnp.repeat(listed, BLOCK, axis=1).astype(jnp.float32)
    panel = l_panel.reshape(NA, S, W).astype(jnp.float32)
    masked = (panel * row_mask.T[:, :, None]).astype(jnp.bfloat16)
    lhat = jnp.einsum("nsw,swv->nsv", masked.astype(jnp.float32), unit_inverse.astype(jnp.float32), precision=lax.Precision.HIGHEST).astype(jnp.bfloat16)
    lhat_flat = lhat.reshape(NA, S * W)
    span = NA // N_PCOL

    def add_range(total, index):
        start = (index * span).astype(jnp.int32)
        cols = lax.dynamic_slice_in_dim(inverse_tile, start, span, 1)
        rows_part = lax.dynamic_slice_in_dim(lhat_flat, start, span, 0)
        partial_value = jnp.dot(cols, rows_part, preferred_element_type=jnp.float32).astype(jnp.bfloat16)
        return total + partial_value.astype(jnp.float32), None

    product, unused = lax.scan(add_range, jnp.zeros((NA, S * W), jnp.float32), jnp.arange(N_PCOL, dtype=jnp.int32))
    wide_mask = jnp.repeat(row_mask, W, axis=0)
    offdiag = -(product.T * wide_mask)
    blocks = product.reshape(NA, S, W)
    total = jnp.einsum("nsv,nsw->svw", blocks, lhat.astype(jnp.float32), precision=lax.Precision.HIGHEST)
    diag = pivot_inverse + total
    return offdiag, diag
```

```python
import jax
import jax.numpy as jnp
from jax import lax
from jax.experimental import pallas as pl
from jax.experimental.pallas import tpu as pltpu
from jax.sharding import PartitionSpec as P

MESH = pl.DeviceIdType.MESH
BLOCK = 128
ORDER = (2, 1, 3, 0)
F32 = jnp.float32
BF16 = jnp.bfloat16


def device(x, y, z, core):
    return ((y % 2) * 4 + x, (y // 2) * 8 + z * 2 + core)


def kernel(
    listed, panel_hbm, tile_hbm, unit, pivot, out, diag_out,
    panel, lhat, tile, mirrored, held, s2, r2, s1, r1, s3, r3, p1, p0, y_send, y_recv,
    kept, split, d_send, d_recv,
    local_sem, core_sem, t_send, t_recv, ye_send, ye_recv, x_send, x_recv, f_send, f_recv,
    z_send, z_recv, yr_send, yr_recv, dg_send, dg_recv,
):
    row, col = lax.axis_index("prow"), lax.axis_index("pcol")
    x, y_lo = row % 4, row // 4
    y_hi, z, core = col // 8, (col // 2) % 4, col % 2
    y = 2 * y_hi + y_lo
    y_swap = 2 * y_lo + y_hi
    rows = panel.shape[0]
    half, quarter, eighth = rows // 2, rows // 4, rows // 8
    blocks = rows // BLOCK

    load_panel = pltpu.make_async_copy(panel_hbm, panel, local_sem.at[0])
    load_panel.start()
    load_tile = pltpu.make_async_copy(tile_hbm, tile.at[core], local_sem.at[1])
    load_tile.start()

    def remote(src, dst, send, recv, to):
        return pltpu.make_async_remote_copy(
            src_ref=src, dst_ref=dst, send_sem=send, recv_sem=recv, device_id=to, device_id_type=MESH
        )

    barrier = pltpu.get_barrier_semaphore()

    def greet(to):
        pl.semaphore_signal(barrier, inc=1, device_id=to, device_id_type=MESH)

    x_next, x_prev = device((x + 1) % 4, y, z, core), device((x + 3) % 4, y, z, core)
    z_next, z_prev = device(x, y, (z + 1) % 4, core), device(x, y, (z + 3) % 4, core)
    y_pair = device(x, 2 * y_hi + 1 - y_lo, z, core)
    y_far = device(x, 2 * (1 - y_hi) + y_lo, z, core)
    other_core = device(x, y, z, 1 - core)
    for step in range(1, 8):
        greet(((row + step) % 8, col))
    for to in (z_next, z_prev, y_far, other_core):
        greet(to)
    for q in range(4):
        greet(device(q, y_swap, x, core))
        greet(device(z, y_swap, q, core))

    load_panel.wait()

    def lhat_block(b, carry):
        at = pl.ds(pl.multiple_of(b * BLOCK, BLOCK), BLOCK)
        mask = listed[col, row * blocks + b].astype(F32)
        masked = (panel[at, :].astype(F32) * mask).astype(BF16)
        lhat[at, :] = jnp.dot(masked, unit[0], preferred_element_type=F32).astype(BF16)
        return carry

    lax.fori_loop(0, blocks, lhat_block, 0)
    pl.semaphore_wait(barrier, 19)

    d_mine = (x + 4 - z) % 4

    def t_copy(q):
        at = pl.ds(q * quarter, quarter)
        return (
            remote(lhat.at[at], mirrored.at[d_mine, y_hi, at], t_send.at[q], t_recv.at[d_mine], device(q, y_swap, x, core)),
            jnp.logical_and(jnp.logical_and(q == x, y_swap == y), x == z),
            at,
        )

    for q in range(4):
        copy, same, at = t_copy(q)

        @pl.when(jnp.logical_not(same))
        def _():
            copy.start()

        @pl.when(same)
        def _():
            mine = pltpu.make_async_copy(lhat.at[at], mirrored.at[d_mine, y_hi, at], local_sem.at[2])
            mine.start()
            mine.wait()

    swap = remote(tile_hbm, tile.at[core], core_sem.at[0], core_sem.at[1], other_core)
    swap.start()

    def quarter_of(d, e, q, part=None):
        if part is None:
            at = pl.ds(pl.multiple_of(q * quarter, quarter), quarter)
        else:
            at = pl.ds(pl.multiple_of(q * quarter + part * eighth, eighth), eighth)
        return mirrored.at[d, e, at]

    lane = (y_lo, 1 - y_lo)
    x_left, x_right, x_far = (x + 3) % 4, (x + 1) % 4, (x + 2) % 4

    def y_copy(d):
        mine = quarter_of(d, lane[0], x)
        return remote(mine, mine, ye_send.at[d], ye_recv.at[d], y_pair)

    def x_copy(d, ab, side):
        mine = quarter_of(d, lane[ab], x)
        to = (x_next, x_prev)[side]
        return remote(mine, mine, x_send.at[d, ab, side], x_recv.at[d, ab, side], to)

    def f_copy(d, ab, side):
        relayed = quarter_of(d, lane[ab], (x_left, x_right)[side], side)
        to = (x_next, x_prev)[side]
        return remote(relayed, relayed, f_send.at[d, ab, side], f_recv.at[d, ab, side], to)

    def arrival(ref, sem):
        return remote(ref, ref, core_sem.at[0], sem, x_next)

    def send_first(d):
        first = quarter_of(d, lane[0], x)
        if d == 0:
            own = jnp.logical_and(y_swap == y, x == z)

            @pl.when(jnp.logical_not(own))
            def _():
                arrival(first, t_recv.at[d]).wait_recv()
        else:
            arrival(first, t_recv.at[d]).wait_recv()
        y_copy(d).start()
        x_copy(d, 0, 0).start()
        x_copy(d, 0, 1).start()

    def send_second(d):
        arrival(quarter_of(d, lane[1], x), ye_recv.at[d]).wait_recv()
        x_copy(d, 1, 0).start()
        x_copy(d, 1, 1).start()

    def relay(d):
        for ab in range(2):
            for side in range(2):
                arrival(quarter_of(d, lane[ab], (x_left, x_right)[side]), x_recv.at[d, ab, side]).wait_recv()
                f_copy(d, ab, side).start()

    def complete(d):
        for ab in range(2):
            for side in range(2):
                arrival(quarter_of(d, lane[ab], x_far, side), f_recv.at[d, ab, side]).wait_recv()

    step_n = 512

    def product(d, start, count, store):
        def body(i, carry):
            at = pl.ds(pl.multiple_of(start + i * step_n, step_n), step_n)
            acc = None
            for k in range(2):
                rhs = jnp.concatenate(
                    [mirrored[d, 0, k * half:(k + 1) * half, :], mirrored[d, 1, k * half:(k + 1) * half, :]], axis=1
                )
                term = jnp.dot(tile[k, at, :], rhs, preferred_element_type=F32)
                acc = term if acc is None else acc + term
            store(i, at, acc)
            return carry

        lax.fori_loop(0, count // step_n, body, 0)

    def z_copy(which, h):
        at = pl.ds(h * half, half)
        src, dst = ((s2, r2), (s1, r1), (s3, r3))[which]
        to = (z_prev, z_next)[h] if which == 0 else (None, z_prev, z_next)[which]
        return remote(src.at[:, at], dst.at[:, at], z_send.at[which, h], z_recv.at[which, h], to)

    def z_arrival(which, h):
        at = pl.ds(h * half, half)
        dst = (r2, r1, r3)[which]
        arrival(dst.at[:, at], z_recv.at[which, h]).wait_recv()

    def into(ref):
        def store(i, at, acc):
            ref[0, at, :] = acc[:, :BLOCK].astype(ref.dtype)
            ref[1, at, :] = acc[:, BLOCK:].astype(ref.dtype)

        return store

    def into_p1(i, at, acc):
        low = pl.ds(pl.multiple_of(i * step_n, step_n), step_n)
        p1[0, low, :] = acc[:, :BLOCK]
        p1[1, low, :] = acc[:, BLOCK:]

    def into_s3_added(i, at, acc):
        s3[0, at, :] = (acc[:, :BLOCK] + r2[0, at, :].astype(F32)).astype(BF16)
        s3[1, at, :] = (acc[:, BLOCK:] + r2[1, at, :].astype(F32)).astype(BF16)

    d0, d1, d2, d3 = ORDER
    send_first(d0)
    send_first(d1)
    send_second(d0)
    relay(d0)
    send_second(d1)
    send_first(d2)
    load_tile.wait()
    swap.wait_recv()
    complete(d0)
    product(d0, 0, half, into(s2))
    z_copy(0, 0).start()
    product(d0, half, half, into(s2))
    z_copy(0, 1).start()

    relay(d1)
    send_second(d2)
    send_first(d3)
    complete(d1)
    product(d1, half, half, into(s1))
    z_copy(1, 1).start()
    product(d1, 0, half, into_p1)

    relay(d2)
    send_second(d3)
    z_arrival(0, 0)
    for e in range(2):
        s1[e, 0:half, :] = (p1[e] + r2[e, 0:half, :].astype(F32)).astype(BF16)
    z_copy(1, 0).start()
    complete(d2)
    z_arrival(0, 1)
    product(d2, half, half, into_s3_added)
    z_copy(2, 1).start()
    product(d2, 0, half, into(s3))
    z_copy(2, 0).start()

    relay(d3)
    complete(d3)
    product(d3, 0, rows, into(p0))

    def y_reduce(h):
        at = pl.ds(h * half, half)
        return remote(y_send.at[at], y_recv.at[at], yr_send.at[h], yr_recv.at[h], y_far)

    for h in (1, 0):
        at = pl.ds(h * half, half)
        z_arrival(1, h)
        z_arrival(2, h)
        e = 1 - y_hi
        y_send[at, :] = (p0[e, at, :] + (r1[e, at, :].astype(F32) + r3[e, at, :].astype(F32))).astype(BF16)
        y_reduce(h).start()
        e = y_hi
        kept[at, :] = p0[e, at, :] + (r1[e, at, :].astype(F32) + r3[e, at, :].astype(F32))

    total = None
    for h in (1, 0):
        arrival(y_recv.at[pl.ds(h * half, half)], yr_recv.at[h]).wait_recv()

        def finish(b, carry):
            at = pl.ds(pl.multiple_of(b * BLOCK, BLOCK), BLOCK)
            value = (kept[at, :] + y_recv[at, :].astype(F32)).T
            mask = listed[col, row * blocks + b].astype(F32)
            out[:, at] = -(value * mask)
            high = value.astype(BF16)
            split[0:BLOCK, at] = high
            split[BLOCK:, at] = (value - high.astype(F32)).astype(BF16)
            return carry

        lax.fori_loop(h * (blocks // 2), (h + 1) * (blocks // 2), finish, 0)
        at = pl.ds(h * half, half)
        both = jnp.dot(split[:, h * half:(h + 1) * half], lhat[at, :], preferred_element_type=F32)
        part = both[0:BLOCK] + both[BLOCK:]
        total = part if total is None else total + part

    d_send[...] = total.astype(BF16)

    def d_copy(step):
        to = (row + step) % 8
        return remote(d_send, d_recv.at[row], dg_send.at[step - 1], dg_recv.at[step - 1], (to, col))

    for step in range(1, 8):
        d_copy(step).start()
    d_recv[row] = d_send[...]
    for step in range(1, 8):
        arrival(d_recv.at[(row + 8 - step) % 8], dg_recv.at[step - 1]).wait_recv()
    total = d_recv[0].astype(F32)
    for other in range(1, 8):
        total = total + d_recv[other].astype(F32)
    diag_out[0] = pivot[0] + total

    swap.wait_send()
    for q in range(4):
        copy, same, at = t_copy(q)

        @pl.when(jnp.logical_not(same))
        def _():
            copy.wait_send()

    for d in range(4):
        y_copy(d).wait_send()
        for ab in range(2):
            for side in range(2):
                x_copy(d, ab, side).wait_send()
                f_copy(d, ab, side).wait_send()
    for which in range(3):
        for h in range(2):
            z_copy(which, h).wait_send()
    for h in range(2):
        y_reduce(h).wait_send()
    for step in range(1, 8):
        d_copy(step).wait_send()


def per_device(l_panel, inverse_tile, unit_inverse, pivot_inverse, listed):
    rows, width = l_panel.shape
    columns = inverse_tile.shape[1]
    dma = pltpu.SemaphoreType.DMA
    vmem = pl.BlockSpec(memory_space=pltpu.VMEM)
    hbm = pl.BlockSpec(memory_space=pltpu.HBM)
    pair = (2, rows, width)
    return pl.pallas_call(
        kernel,
        out_shape=(
            jax.ShapeDtypeStruct((width, rows), F32),
            jax.ShapeDtypeStruct((1, width, width), F32),
        ),
        in_specs=[pl.BlockSpec(memory_space=pltpu.SMEM), hbm, hbm, vmem, vmem],
        out_specs=(vmem, vmem),
        scratch_shapes=[
            pltpu.VMEM((rows, width), BF16),
            pltpu.VMEM((rows, width), BF16),
            pltpu.VMEM((2, rows, columns), BF16),
            pltpu.VMEM((4, 2, rows, width), BF16),
            pltpu.VMEM((8, width), BF16),
            pltpu.VMEM(pair, BF16),
            pltpu.VMEM(pair, BF16),
            pltpu.VMEM(pair, BF16),
            pltpu.VMEM(pair, BF16),
            pltpu.VMEM(pair, BF16),
            pltpu.VMEM(pair, BF16),
            pltpu.VMEM((2, rows // 2, width), F32),
            pltpu.VMEM(pair, F32),
            pltpu.VMEM((rows, width), BF16),
            pltpu.VMEM((rows, width), BF16),
            pltpu.VMEM((rows, width), F32),
            pltpu.VMEM((2 * width, rows), BF16),
            pltpu.VMEM((width, width), BF16),
            pltpu.VMEM((8, width, width), BF16),
            dma((3,)),
            dma((2,)),
            dma((4,)),
            dma((4,)),
            dma((4,)),
            dma((4,)),
            dma((4, 2, 2)),
            dma((4, 2, 2)),
            dma((4, 2, 2)),
            dma((4, 2, 2)),
            dma((3, 2)),
            dma((3, 2)),
            dma((2,)),
            dma((2,)),
            dma((7,)),
            dma((7,)),
        ],
        compiler_params=pltpu.CompilerParams(
            collective_id=0, has_side_effects=True, vmem_limit_bytes=48 << 20
        ),
    )(listed, l_panel, inverse_tile, unit_inverse, pivot_inverse)


def solution(mesh):
    return jax.shard_map(
        per_device,
        mesh=mesh,
        in_specs=(
            P("prow", "pcol"),
            P("prow", "pcol"),
            P("pcol", None, None),
            P("pcol", None, None),
            P(),
        ),
        out_specs=(P("pcol", "prow"), P("pcol", None, None)),
        check_vma=False,
    )
```

```python
import jax
import jax.numpy as jnp
from jax import lax
from jax.experimental import pallas as pl
from jax.experimental.pallas import tpu as pltpu
from jax.sharding import PartitionSpec as P

MESH = pl.DeviceIdType.MESH
BLOCK = 128
CHUNKS = ((2, 0), (2, 1), (1, 1), (3, 1), (1, 0), (3, 0), (0, 1), (0, 0))
F32 = jnp.float32
BF16 = jnp.bfloat16


def device(x, y, z, core):
    return ((y % 2) * 4 + x, (y // 2) * 8 + z * 2 + core)


def kernel(
    listed_hbm, panel_hbm, tile_hbm, unit_hbm, pivot_hbm, out, diag_out,
    listed, unit, pivot, panel, lhat, tile, mirrored, s2, r2, s1, r1, s3, r3, p1, p3, p0, y_send, y_recv,
    split, d_send, d_recv,
    local_sem, core_sem, t_send, in_recv, ye_send, x_send, x_recv, f_send, f_recv,
    z_send, z_recv, yr_send, yr_recv, dg_send, dg_recv,
):
    row, col = lax.axis_index("prow"), lax.axis_index("pcol")
    x, y_lo = row % 4, row // 4
    y_hi, z, core = col // 8, (col // 2) % 4, col % 2
    y = 2 * y_hi + y_lo
    y_swap = 2 * y_lo + y_hi
    rows = panel.shape[0]
    half, quarter, eighth = rows // 2, rows // 4, rows // 8
    blocks = rows // BLOCK

    loads = [
        pltpu.make_async_copy(src, dst, local_sem.at[i])
        for i, (src, dst) in enumerate(
            (
                (panel_hbm, panel),
                (listed_hbm, listed),
                (unit_hbm, unit),
                (tile_hbm, tile.at[core]),
                (pivot_hbm, pivot),
            )
        )
    ]
    for load in loads:
        load.start()

    def remote(src, dst, send, recv, to):
        return pltpu.make_async_remote_copy(
            src_ref=src, dst_ref=dst, send_sem=send, recv_sem=recv, device_id=to, device_id_type=MESH
        )

    barrier = pltpu.get_barrier_semaphore()

    def greet(to):
        pl.semaphore_signal(barrier, inc=1, device_id=to, device_id_type=MESH)

    x_next, x_prev = device((x + 1) % 4, y, z, core), device((x + 3) % 4, y, z, core)
    z_next, z_prev = device(x, y, (z + 1) % 4, core), device(x, y, (z + 3) % 4, core)
    y_pair = device(x, 2 * y_hi + 1 - y_lo, z, core)
    y_far = device(x, 2 * (1 - y_hi) + y_lo, z, core)
    other_core = device(x, y, z, 1 - core)
    for step in range(1, 8):
        greet(((row + step) % 8, col))
    for to in (z_next, z_prev, y_far, other_core):
        greet(to)
    for q in range(4):
        greet(device(q, y_swap, x, core))
        greet(device(z, y_swap, q, core))

    for load in loads[:3]:
        load.wait()

    def lhat_block(b, carry):
        at = pl.ds(pl.multiple_of(b * BLOCK, BLOCK), BLOCK)
        mask = listed[col, row * blocks + b].astype(F32)
        masked = (panel[at, :].astype(F32) * mask).astype(BF16)
        lhat[at, :] = jnp.dot(masked, unit[0], preferred_element_type=F32).astype(BF16)
        return carry

    lax.fori_loop(0, blocks, lhat_block, 0)
    pl.semaphore_wait(barrier, 19)

    d_mine = (x + 4 - z) % 4

    def t_copy(q):
        at = pl.ds(q * quarter, quarter)
        same = jnp.logical_and(jnp.logical_and(q == x, y_swap == y), x == z)
        src, dst, sem = lhat.at[at], mirrored.at[d_mine, y_hi, at], in_recv.at[d_mine, y_hi]
        return remote(src, dst, t_send.at[q], sem, device(q, y_swap, x, core)), same, (src, dst, sem)

    for q in range(4):
        copy, same, (src, dst, sem) = t_copy(q)

        @pl.when(jnp.logical_not(same))
        def _():
            copy.start()

        @pl.when(same)
        def _():
            pltpu.make_async_copy(src, dst, sem).start()

    swap = remote(tile_hbm, tile.at[core], core_sem.at[0], core_sem.at[1], other_core)
    swap.start()

    def quarter_of(d, e, q, part=None):
        if part is None:
            at = pl.ds(pl.multiple_of(q * quarter, quarter), quarter)
        else:
            at = pl.ds(pl.multiple_of(q * quarter + part * eighth, eighth), eighth)
        return mirrored.at[d, e, at]

    lane = (y_hi, 1 - y_hi)
    x_left, x_right, x_far = (x + 3) % 4, (x + 1) % 4, (x + 2) % 4

    def y_copy(d, nf):
        mine = quarter_of(d, lane[nf], x)
        return remote(mine, mine, ye_send.at[d], in_recv.at[d, lane[nf]], y_pair)

    def x_copy(d, nf, side):
        mine = quarter_of(d, lane[nf], x)
        to = (x_next, x_prev)[side]
        return remote(mine, mine, x_send.at[d, nf, side], x_recv.at[d, nf, side], to)

    def f_copy(d, nf, side):
        relayed = quarter_of(d, lane[nf], (x_left, x_right)[side], side)
        to = (x_next, x_prev)[side]
        return remote(relayed, relayed, f_send.at[d, nf, side], f_recv.at[d, nf, side], to)

    def arrival(ref, sem):
        return remote(ref, ref, core_sem.at[0], sem, x_next)

    def enter(d, nf):
        arrival(quarter_of(d, lane[nf], x), in_recv.at[d, lane[nf]]).wait_recv()

        @pl.when(y_lo == lane[nf])
        def _():
            y_copy(d, nf).start()

        x_copy(d, nf, 0).start()
        x_copy(d, nf, 1).start()

    def relay(d, nf):
        for side in range(2):
            arrival(quarter_of(d, lane[nf], (x_left, x_right)[side]), x_recv.at[d, nf, side]).wait_recv()
            f_copy(d, nf, side).start()

    def complete(d, nf):
        for side in range(2):
            arrival(quarter_of(d, lane[nf], x_far, side), f_recv.at[d, nf, side]).wait_recv()

    step_n = 512

    def product(d, nf, start, count, store):
        def body(i, carry):
            at = pl.ds(pl.multiple_of(start + i * step_n, step_n), step_n)
            acc = None
            for k in range(2):
                rhs = mirrored[d, lane[nf], k * half:(k + 1) * half, :]
                term = jnp.dot(tile[k, at, :], rhs, preferred_element_type=F32)
                acc = term if acc is None else acc + term
            store(i, at, acc)
            return carry

        lax.fori_loop(0, count // step_n, body, 0)

    sides = {2: (s2, r2), 1: (s1, r1), 3: (s3, r3)}

    def z_copy(d, nf, h):
        at = pl.ds(h * half, half)
        src, dst = sides[d]
        to = (z_prev, z_next)[h] if d == 2 else (z_prev if d == 1 else z_next)
        return remote(src.at[nf, at], dst.at[nf, at], z_send.at[d - 1, nf, h], z_recv.at[d - 1, nf, h], to)

    def z_arrival(d, nf, h):
        arrival(sides[d][1].at[nf, pl.ds(h * half, half)], z_recv.at[d - 1, nf, h]).wait_recv()

    def into(ref, nf):
        def store(i, at, acc):
            ref[nf, at, :] = acc.astype(ref.dtype)

        return store

    def into_half(ref, nf):
        def store(i, at, acc):
            ref[nf, pl.ds(pl.multiple_of(i * step_n, step_n), step_n), :] = acc

        return store

    def compute(d, nf):
        if d == 2:
            for h in range(2):
                product(d, nf, h * half, half, into(s2, nf))
                z_copy(d, nf, h).start()
        elif d == 1:
            product(d, nf, half, half, into(s1, nf))
            z_copy(d, nf, 1).start()
            product(d, nf, 0, half, into_half(p1, nf))
        elif d == 3:
            product(d, nf, 0, half, into(s3, nf))
            z_copy(d, nf, 0).start()
            product(d, nf, half, half, into_half(p3, nf))
        else:
            product(d, nf, 0, rows, into(p0, nf))

    def add_far(d, nf):
        h = 0 if d == 1 else 1
        at = pl.ds(h * half, half)
        z_arrival(2, nf, h)
        held = p1 if d == 1 else p3
        sides[d][0][nf, at, :] = (held[nf] + r2[nf, at, :].astype(F32)).astype(BF16)
        z_copy(d, nf, h).start()

    enter(*CHUNKS[0])
    enter(*CHUNKS[1])
    for i, (d, nf) in enumerate(CHUNKS):
        relay(d, nf)
        if i + 2 < len(CHUNKS):
            enter(*CHUNKS[i + 2])
        if i == 0:
            loads[3].wait()
            swap.wait_recv()
        if i == 4:
            add_far(1, 1)
            add_far(3, 1)
        if i == 7:
            for h in range(2):
                z_arrival(1, 1, h)
                z_arrival(3, 1, h)
            y_send[...] = (p0[1] + (r1[1].astype(F32) + r3[1].astype(F32))).astype(BF16)
            y_reduce = remote(y_send, y_recv, yr_send.at[0], yr_recv.at[0], y_far)
            y_reduce.start()
        complete(d, nf)
        compute(d, nf)
        if (d, nf) in ((1, 0), (3, 0)):
            add_far(d, nf)

    for h in (1, 0):
        z_arrival(1, 0, h)
        z_arrival(3, 0, h)
    arrival(y_recv, yr_recv.at[0]).wait_recv()

    def finish(b, carry):
        at = pl.ds(pl.multiple_of(b * BLOCK, BLOCK), BLOCK)
        value = (p0[0, at, :] + y_recv[at, :].astype(F32)) + (r1[0, at, :].astype(F32) + r3[0, at, :].astype(F32))
        value = value.T
        mask = listed[col, row * blocks + b].astype(F32)
        out[:, at] = -(value * mask)
        high = value.astype(BF16)
        split[0:BLOCK, at] = high
        split[BLOCK:, at] = (value - high.astype(F32)).astype(BF16)
        return carry

    lax.fori_loop(0, blocks, finish, 0)
    both = jnp.dot(split[...], lhat[...], preferred_element_type=F32)
    total = both[0:BLOCK] + both[BLOCK:]
    d_send[...] = total.astype(BF16)

    def d_copy(step):
        to = (row + step) % 8
        return remote(d_send, d_recv.at[row], dg_send.at[step - 1], dg_recv.at[step - 1], (to, col))

    for step in range(1, 8):
        d_copy(step).start()
    d_recv[row] = d_send[...]
    for step in range(1, 8):
        arrival(d_recv.at[(row + 8 - step) % 8], dg_recv.at[step - 1]).wait_recv()
    total = d_recv[0].astype(F32)
    for other in range(1, 8):
        total = total + d_recv[other].astype(F32)
    loads[4].wait()
    diag_out[0] = pivot[0] + total

    swap.wait_send()
    for q in range(4):
        copy, same, _ = t_copy(q)

        @pl.when(jnp.logical_not(same))
        def _():
            copy.wait_send()

    for d, nf in CHUNKS:

        @pl.when(y_lo == lane[nf])
        def _():
            y_copy(d, nf).wait_send()

        for side in range(2):
            x_copy(d, nf, side).wait_send()
            f_copy(d, nf, side).wait_send()
            if d:
                z_copy(d, nf, side).wait_send()
    y_reduce.wait_send()
    for step in range(1, 8):
        d_copy(step).wait_send()


def per_device(l_panel, inverse_tile, unit_inverse, pivot_inverse, listed):
    rows, width = l_panel.shape
    columns = inverse_tile.shape[1]
    dma = pltpu.SemaphoreType.DMA
    vmem = pl.BlockSpec(memory_space=pltpu.VMEM)
    hbm = pl.BlockSpec(memory_space=pltpu.HBM)
    pair = (2, rows, width)
    operands = (listed, l_panel, inverse_tile, unit_inverse, pivot_inverse)
    return pl.pallas_call(
        kernel,
        out_shape=(
            jax.ShapeDtypeStruct((width, rows), F32),
            jax.ShapeDtypeStruct((1, width, width), F32),
        ),
        in_specs=[hbm] * 5,
        out_specs=(vmem, vmem),
        scratch_shapes=[
            pltpu.SMEM(listed.shape, jnp.int32),
            pltpu.VMEM((1, width, width), BF16),
            pltpu.VMEM((1, width, width), F32),
            pltpu.VMEM((rows, width), BF16),
            pltpu.VMEM((rows, width), BF16),
            pltpu.VMEM((2, rows, columns), BF16),
            pltpu.VMEM((4, 2, rows, width), BF16),
            pltpu.VMEM(pair, BF16),
            pltpu.VMEM(pair, BF16),
            pltpu.VMEM(pair, BF16),
            pltpu.VMEM(pair, BF16),
            pltpu.VMEM(pair, BF16),
            pltpu.VMEM(pair, BF16),
            pltpu.VMEM((2, rows // 2, width), F32),
            pltpu.VMEM((2, rows // 2, width), F32),
            pltpu.VMEM(pair, F32),
            pltpu.VMEM((rows, width), BF16),
            pltpu.VMEM((rows, width), BF16),
            pltpu.VMEM((2 * width, rows), BF16),
            pltpu.VMEM((width, width), BF16),
            pltpu.VMEM((8, width, width), BF16),
            dma((5,)),
            dma((2,)),
            dma((4,)),
            dma((4, 2)),
            dma((4,)),
            dma((4, 2, 2)),
            dma((4, 2, 2)),
            dma((4, 2, 2)),
            dma((4, 2, 2)),
            dma((3, 2, 2)),
            dma((3, 2, 2)),
            dma((1,)),
            dma((1,)),
            dma((7,)),
            dma((7,)),
        ],
        compiler_params=pltpu.CompilerParams(
            collective_id=0, has_side_effects=True, vmem_limit_bytes=60 << 20
        ),
    )(*(pltpu.with_memory_space_constraint(a, pltpu.HBM) for a in operands))


def solution(mesh):
    return jax.shard_map(
        per_device,
        mesh=mesh,
        in_specs=(
            P("prow", "pcol"),
            P("prow", "pcol"),
            P("pcol", None, None),
            P("pcol", None, None),
            P(),
        ),
        out_specs=(P("pcol", "prow"), P("pcol", None, None)),
        check_vma=False,
    )
```

```python
import jax
import jax.numpy as jnp
from jax import lax
from jax.experimental import pallas as pl
from jax.experimental.pallas import tpu as pltpu
from jax.sharding import PartitionSpec as P

MESH = pl.DeviceIdType.MESH
BLOCK = 128
STEP = 512
ORDER = ((2, 0), (2, 1), (1, 1), (3, 1), (0, 1), (1, 0), (3, 0), (0, 0))
ADDED = {3: 2, 4: 3, 5: 5, 6: 6}
Y_AT = 7
F32 = jnp.float32
BF16 = jnp.bfloat16


def device(x, y, z, core):
    return ((y % 2) * 4 + x, (y // 2) * 8 + z * 2 + core)


def pick(index, table):
    value = table[-1]
    for at in range(len(table) - 2, -1, -1):
        value = jnp.where(index == at, table[at], value)
    return value


def chunk(index):
    return pick(index, [d for d, _ in ORDER]), pick(index, [nf for _, nf in ORDER])


def kernel(
    listed_hbm, panel_hbm, tile_hbm, unit_hbm, pivot_hbm, out, diag_out,
    listed, unit, pivot, panel, lhat, tile, mirrored, part, heard, y_send, y_recv,
    stage, split, d_send, d_recv,
    local_sem, core_sem, t_send, td_send, t_recv, in_recv, sw_send, ye_send,
    x_send, x_recv, f_send, f_recv, z_send, z_recv, yr_send, yr_recv, dg_send, dg_recv,
):
    row, col = lax.axis_index("prow"), lax.axis_index("pcol")
    x, y_lo = row % 4, row // 4
    y_hi, z, core = col // 8, (col // 2) % 4, col % 2
    y = 2 * y_hi + y_lo
    y_swap = 2 * y_lo + y_hi
    y_other = 2 * y_hi + 1 - y_lo
    stays = y_lo == y_hi
    moves = y_lo != y_hi
    rows = panel.shape[0]
    half, quarter, eighth = rows // 2, rows // 4, rows // 8
    blocks = rows // BLOCK

    loads = [
        pltpu.make_async_copy(src, dst, local_sem.at[i])
        for i, (src, dst) in enumerate(
            (
                (panel_hbm, panel),
                (listed_hbm, listed),
                (unit_hbm, unit),
                (tile_hbm, tile.at[core]),
                (pivot_hbm, pivot),
            )
        )
    ]
    for load in loads:
        load.start()

    def remote(src, dst, send, recv, to):
        return pltpu.make_async_remote_copy(
            src_ref=src, dst_ref=dst, send_sem=send, recv_sem=recv, device_id=to, device_id_type=MESH
        )

    def each(count, body):
        def step(i, carry):
            body(i)
            return carry

        lax.fori_loop(0, count, step, 0)

    def span(start, size):
        return pl.ds(pl.multiple_of(start, size), size)

    barrier = pltpu.get_barrier_semaphore()

    def greet(to):
        pl.semaphore_signal(barrier, inc=1, device_id=to, device_id_type=MESH)

    y_pair = device(x, y_other, z, core)
    y_far = device(x, 2 * (1 - y_hi) + y_lo, z, core)
    other_core = device(x, y, z, 1 - core)
    swapped = device(x, y_swap, z, core)
    for step in range(1, 8):
        greet(((row + step) % 8, col))
    for to in (device(x, y, (z + 1) % 4, core), device(x, y, (z + 3) % 4, core), y_far, other_core, swapped):
        greet(to)

    def greet_group(q):
        greet(device(q, y, x, core))
        greet(device(z, y, q, core))
        greet(device(q, y_other, x, core))
        greet(device(z, y_other, q, core))

    each(4, greet_group)

    for load in loads[:3]:
        load.wait()

    def lhat_block(b):
        at = span(b * BLOCK, BLOCK)
        mask = listed[col, row * blocks + b].astype(F32)
        masked = (panel[at, :].astype(F32) * mask).astype(BF16)
        lhat[at, :] = jnp.dot(masked, unit[0], preferred_element_type=F32).astype(BF16)

    each(blocks, lhat_block)
    pl.semaphore_wait(barrier, 28)

    d_mine = (x + 4 - z) % 4
    twice = jnp.logical_and(stays, d_mine == 2)

    def t_copy(q, straight):
        at = span(q * quarter, quarter)
        if straight:
            dst, sem = mirrored.at[d_mine, y_hi, at], in_recv.at[d_mine, y_hi]
        else:
            dst, sem = stage.at[d_mine], t_recv.at[d_mine]
        return remote(lhat.at[at], dst, t_send.at[q], sem, device(q, y, x, core)), (lhat.at[at], dst, sem)

    def t_twice(q):
        at = span(q * quarter, quarter)
        to = device(q, y_other, x, core)
        return remote(lhat.at[at], mirrored.at[2, y_hi, at], td_send.at[q], in_recv.at[2, y_hi], to)

    for straight, when in ((True, stays), (False, moves)):

        @pl.when(when)
        def _():
            @pl.when(x == z)
            def _():
                _, (src, dst, sem) = t_copy(x, straight)
                pltpu.make_async_copy(src, dst, sem).start()

            def send(q):
                @pl.when(jnp.logical_or(q != x, x != z))
                def _():
                    t_copy(q, straight)[0].start()

            each(4, send)

    @pl.when(twice)
    def _():
        each(4, lambda q: t_twice(q).start())

    swap = remote(tile_hbm, tile.at[core], core_sem.at[0], core_sem.at[1], other_core)
    swap.start()

    def quarter_of(d, e, q):
        return mirrored.at[d, e, span(q * quarter, quarter)]

    def eighth_of(d, e, q, side):
        return mirrored.at[d, e, span(q * quarter + side * eighth, eighth)]

    def lane(nf):
        return jnp.where(nf == 0, y_hi, 1 - y_hi)

    def side_x(side):
        return (x + 1 + 2 * side) % 4

    def from_x(side):
        return (x + 3 + 2 * side) % 4

    def swap_copy(d):
        return remote(stage.at[d], quarter_of(d, y_hi, x), sw_send.at[d], in_recv.at[d, y_hi], swapped)

    def y_copy(d):
        mine = quarter_of(d, y_lo, x)
        return remote(mine, mine, ye_send.at[d], in_recv.at[d, y_lo], y_pair)

    def x_copy(d, nf, side):
        mine = quarter_of(d, lane(nf), x)
        to = device(side_x(side), y, z, core)
        return remote(mine, mine, x_send.at[d, nf, side], x_recv.at[d, nf, side], to)

    def f_copy(d, nf, side):
        relayed = eighth_of(d, lane(nf), from_x(side), side)
        to = device(side_x(side), y, z, core)
        return remote(relayed, relayed, f_send.at[d, nf, side], f_recv.at[d, nf, side], to)

    def arrival(ref, sem):
        return remote(ref, ref, core_sem.at[0], sem, y_far)

    def y_sends(d):
        return jnp.logical_not(jnp.logical_and(stays, d == 2))

    def enter(index):
        d, nf = chunk(index)
        e = lane(nf)
        arrival(quarter_of(d, e, x), in_recv.at[d, e]).wait_recv()

        @pl.when(jnp.logical_and(y_lo == e, y_sends(d)))
        def _():
            y_copy(d).start()

        for side in range(2):
            x_copy(d, nf, side).start()

    def relay(index):
        d, nf = chunk(index)
        for side in range(2):
            arrival(quarter_of(d, lane(nf), from_x(side)), x_recv.at[d, nf, side]).wait_recv()
            f_copy(d, nf, side).start()

    def complete(d, nf):
        for side in range(2):
            arrival(eighth_of(d, lane(nf), (x + 2) % 4, side), f_recv.at[d, nf, side]).wait_recv()

    def z_copy(d, nf, h):
        at = span(h * half, half)
        down = jnp.logical_or(d == 1, jnp.logical_and(d == 2, h == 0))
        to = device(x, y, (z + jnp.where(down, 3, 1)) % 4, core)
        return remote(part.at[d, nf, at], heard.at[d - 1, nf, at], z_send.at[d, nf, h], z_recv.at[d - 1, nf, h], to)

    def z_arrival(d, nf, h):
        arrival(heard.at[d - 1, nf, span(h * half, half)], z_recv.at[d - 1, nf, h]).wait_recv()

    def y_reduce(h):
        at = span(h * half, half)
        return remote(y_send.at[at], y_recv.at[at], yr_send.at[h], yr_recv.at[h], y_far)

    def send_far(j):
        h = 1 - j
        z_arrival(1, 1, h)
        z_arrival(3, 1, h)

        def add(i):
            at = span(h * half + i * BLOCK, BLOCK)
            far = part[0, 1, at, :].astype(F32) + (heard[0, 1, at, :].astype(F32) + heard[2, 1, at, :].astype(F32))
            y_send[at, :] = far.astype(BF16)

        each(half // BLOCK, add)
        y_reduce(h).start()

    def add_heard(index):
        d, nf = chunk(index)
        h = jnp.where(d == 1, 0, 1)
        z_arrival(2, nf, h)

        def add(i):
            at = span(h * half + i * BLOCK, BLOCK)
            part[d, nf, at, :] = (part[d, nf, at, :].astype(F32) + heard[1, nf, at, :].astype(F32)).astype(BF16)

        each(half // BLOCK, add)
        z_copy(d, nf, h).start()

    @pl.when(moves)
    def _():
        def move(i):
            d = pick(i, (2, 1, 3, 0))
            arrival(stage.at[d], t_recv.at[d]).wait_recv()
            swap_copy(d).start()

        each(4, move)

    enter(0)
    relay(0)
    enter(1)
    enter(2)

    def half_chunk(t):
        i, first = t // 2, t % 2 == 0
        d, nf = chunk(i)
        h = jnp.where(d == 3, t % 2, 1 - t % 2)

        @pl.when(jnp.logical_and(first, i < 7))
        def _():
            relay(i + 1)

        @pl.when(t == 2 * Y_AT)
        def _():
            each(2, send_far)

        @pl.when(first)
        def _():
            complete(d, nf)

        @pl.when(t == 0)
        def _():
            loads[3].wait()
            swap.wait_recv()

        e = lane(nf)

        def product(j):
            at = span(h * half + j * STEP, STEP)
            acc = jnp.dot(tile[0, at, :], mirrored[d, e, 0:half, :], preferred_element_type=F32)
            acc += jnp.dot(tile[1, at, :], mirrored[d, e, half:, :], preferred_element_type=F32)
            part[d, nf, at, :] = acc.astype(BF16)

        each(half // STEP, product)

        @pl.when(jnp.logical_or(d == 2, jnp.logical_and(first, d != 0)))
        def _():
            z_copy(d, nf, h).start()

        @pl.when(jnp.logical_and(first, i < 5))
        def _():
            enter(i + 3)

        added = pick(i, [ADDED.get(k, -1) for k in range(8)])

        @pl.when(jnp.logical_and(jnp.logical_not(first), added >= 0))
        def _():
            add_heard(added)

    each(16, half_chunk)

    total = None
    for h in (1, 0):
        arrival(y_recv.at[span(h * half, half)], yr_recv.at[h]).wait_recv()
        z_arrival(1, 0, h)
        z_arrival(3, 0, h)

        def finish(b):
            at = span((b + h * (blocks // 2)) * BLOCK, BLOCK)
            value = part[0, 0, at, :].astype(F32) + y_recv[at, :].astype(F32)
            value = (value + (heard[0, 0, at, :].astype(F32) + heard[2, 0, at, :].astype(F32))).T
            mask = listed[col, row * blocks + b + h * (blocks // 2)].astype(F32)
            out[:, at] = -(value * mask)
            high = value.astype(BF16)
            split[0:BLOCK, at] = high
            split[BLOCK:, at] = (value - high.astype(F32)).astype(BF16)

        each(blocks // 2, finish)
        both = jnp.dot(split[:, h * half:(h + 1) * half], lhat[h * half:(h + 1) * half, :], preferred_element_type=F32)
        both = both[0:BLOCK] + both[BLOCK:]
        total = both if total is None else total + both

    d_send[...] = total.astype(BF16)

    def d_copy(step):
        to = (row + step + 1) % 8
        return remote(d_send, d_recv.at[row], dg_send.at[step], dg_recv.at[step], (to, col))

    each(7, lambda step: d_copy(step).start())
    d_recv[row] = d_send[...]
    each(7, lambda step: arrival(d_recv.at[(row + 7 - step) % 8], dg_recv.at[step]).wait_recv())
    total = d_recv[0].astype(F32)
    for other in range(1, 8):
        total = total + d_recv[other].astype(F32)
    loads[4].wait()
    diag_out[0] = pivot[0] + total

    swap.wait_send()
    for straight, when in ((True, stays), (False, moves)):

        @pl.when(when)
        def _():
            def sent(q):
                @pl.when(jnp.logical_or(q != x, x != z))
                def _():
                    t_copy(q, straight)[0].wait_send()

            each(4, sent)

    @pl.when(twice)
    def _():
        each(4, lambda q: t_twice(q).wait_send())

    def sent(d):
        @pl.when(moves)
        def _():
            swap_copy(d).wait_send()

        @pl.when(y_sends(d))
        def _():
            y_copy(d).wait_send()

        def sides(j):
            nf, side = j // 2, j % 2
            x_copy(d, nf, side).wait_send()
            f_copy(d, nf, side).wait_send()

            @pl.when(d != 0)
            def _():
                z_copy(d, nf, side).wait_send()

        each(4, sides)

    each(4, sent)
    each(2, lambda h: y_reduce(h).wait_send())
    each(7, lambda step: d_copy(step).wait_send())


def per_device(l_panel, inverse_tile, unit_inverse, pivot_inverse, listed):
    rows, width = l_panel.shape
    columns = inverse_tile.shape[1]
    dma = pltpu.SemaphoreType.DMA
    vmem = pl.BlockSpec(memory_space=pltpu.VMEM)
    hbm = pl.BlockSpec(memory_space=pltpu.HBM)
    operands = (listed, l_panel, inverse_tile, unit_inverse, pivot_inverse)
    return pl.pallas_call(
        kernel,
        out_shape=(
            jax.ShapeDtypeStruct((width, rows), F32),
            jax.ShapeDtypeStruct((1, width, width), F32),
        ),
        in_specs=[hbm] * 5,
        out_specs=(vmem, vmem),
        scratch_shapes=[
            pltpu.SMEM(listed.shape, jnp.int32),
            pltpu.VMEM((1, width, width), BF16),
            pltpu.VMEM((1, width, width), F32),
            pltpu.VMEM((rows, width), BF16),
            pltpu.VMEM((rows, width), BF16),
            pltpu.VMEM((2, rows, columns), BF16),
            pltpu.VMEM((4, 2, rows, width), BF16),
            pltpu.VMEM((4, 2, rows, width), BF16),
            pltpu.VMEM((3, 2, rows, width), BF16),
            pltpu.VMEM((rows, width), BF16),
            pltpu.VMEM((rows, width), BF16),
            pltpu.VMEM((4, rows // 4, width), BF16),
            pltpu.VMEM((2 * width, rows), BF16),
            pltpu.VMEM((width, width), BF16),
            pltpu.VMEM((8, width, width), BF16),
            dma((5,)),
            dma((2,)),
            dma((4,)),
            dma((4,)),
            dma((4,)),
            dma((4, 2)),
            dma((4,)),
            dma((4,)),
            dma((4, 2, 2)),
            dma((4, 2, 2)),
            dma((4, 2, 2)),
            dma((4, 2, 2)),
            dma((4, 2, 2)),
            dma((3, 2, 2)),
            dma((2,)),
            dma((2,)),
            dma((7,)),
            dma((7,)),
        ],
        compiler_params=pltpu.CompilerParams(
            collective_id=0, has_side_effects=True, vmem_limit_bytes=36 << 20
        ),
    )(*(pltpu.with_memory_space_constraint(a, pltpu.HBM) for a in operands))


def solution(mesh):
    return jax.shard_map(
        per_device,
        mesh=mesh,
        in_specs=(
            P("prow", "pcol"),
            P("prow", "pcol"),
            P("pcol", None, None),
            P("pcol", None, None),
            P(),
        ),
        out_specs=(P("pcol", "prow"), P("pcol", None, None)),
        check_vma=False,
    )
```

```python
import jax
import jax.numpy as jnp
from jax import lax
from jax.experimental import pallas as pl
from jax.experimental.pallas import tpu as pltpu
from jax.sharding import PartitionSpec as P

MESH = pl.DeviceIdType.MESH
BLOCK = 128
STEP = 1024
ORDER = (
    ((2, 0), (2, 1), (1, 1), (3, 1), (0, 0), (0, 1), (1, 0), (3, 0)),
    ((2, 1), (2, 0), (1, 1), (3, 1), (0, 1), (0, 0), (1, 0), (3, 0)),
)
ADDED = ({7: 2, 9: 3, 13: 6, 14: 7}, {7: 2, 9: 3, 13: 6, 14: 7})
Y_AT = 7
AHEAD = 4
F32 = jnp.float32
BF16 = jnp.bfloat16


def device(x, y, z, core):
    return ((y % 2) * 4 + x, (y // 2) * 8 + z * 2 + core)


def pick(index, table):
    value = table[-1]
    for at in range(len(table) - 2, -1, -1):
        value = jnp.where(index == at, table[at], value)
    return value


def kernel(
    listed_hbm, panel_hbm, tile_hbm, unit_hbm, pivot_hbm, out, diag_out,
    listed, unit, pivot, panel, lhat, tile, mirrored, part, heard, y_send, y_recv,
    stage, split, d_send, d_recv,
    local_sem, core_sem, t_send, t_recv, in_recv, sw_send, ye_send,
    x_send, x_recv, f_send, f_recv, z_send, z_recv, p_send, p_recv, yr_send, yr_recv, dg_send, dg_recv,
):
    row, col = lax.axis_index("prow"), lax.axis_index("pcol")
    x, y_lo = row % 4, row // 4
    y_hi, z, core = col // 8, (col // 2) % 4, col % 2
    y = 2 * y_hi + y_lo
    y_swap = 2 * y_lo + y_hi
    y_other = 2 * y_hi + 1 - y_lo
    stays = y_lo == y_hi
    moves = y_lo != y_hi

    def choose(index, tables):
        return jnp.where(stays, pick(index, tables[0]), pick(index, tables[1]))

    def chunk(index):
        return tuple(choose(index, [[c[k] for c in order] for order in ORDER]) for k in range(2))

    rows = panel.shape[0]
    half, quarter, eighth = rows // 2, rows // 4, rows // 8
    blocks = rows // BLOCK

    loads = [
        pltpu.make_async_copy(src, dst, local_sem.at[i])
        for i, (src, dst) in enumerate(
            (
                (panel_hbm, panel),
                (listed_hbm, listed),
                (unit_hbm, unit),
                (tile_hbm, tile.at[core]),
                (pivot_hbm, pivot),
            )
        )
    ]
    for load in loads:
        load.start()

    def remote(src, dst, send, recv, to):
        return pltpu.make_async_remote_copy(
            src_ref=src, dst_ref=dst, send_sem=send, recv_sem=recv, device_id=to, device_id_type=MESH
        )

    def each(count, body):
        def step(i, carry):
            body(i)
            return carry

        lax.fori_loop(0, count, step, 0)

    def span(start, size):
        return pl.ds(pl.multiple_of(start, size), size)

    barrier = pltpu.get_barrier_semaphore()

    def greet(to):
        pl.semaphore_signal(barrier, inc=1, device_id=to, device_id_type=MESH)

    y_pair = device(x, y_other, z, core)
    y_far = device(x, 2 * (1 - y_hi) + y_lo, z, core)
    other_core = device(x, y, z, 1 - core)
    swapped = device(x, y_swap, z, core)
    for step in range(1, 8):
        greet(((row + step) % 8, col))
    for to in (device(x, y, (z + 1) % 4, core), device(x, y, (z + 3) % 4, core), y_far, other_core, swapped):
        greet(to)

    def greet_group(q):
        greet(device(q, y, x, core))
        greet(device(z, y, q, core))

    each(4, greet_group)

    for load in loads[:3]:
        load.wait()

    def lhat_block(b):
        at = span(b * BLOCK, BLOCK)
        mask = listed[col, row * blocks + b].astype(F32)
        masked = (panel[at, :].astype(F32) * mask).astype(BF16)
        lhat[at, :] = jnp.dot(masked, unit[0], preferred_element_type=F32).astype(BF16)

    each(blocks, lhat_block)
    pl.semaphore_wait(barrier, 20)

    d_mine = (x + 4 - z) % 4

    def t_copy(q, straight):
        at = span(q * quarter, quarter)
        if straight:
            dst, sem = mirrored.at[d_mine, y_hi, at], in_recv.at[d_mine, y_hi]
        else:
            dst, sem = stage.at[d_mine], t_recv.at[d_mine]
        return remote(lhat.at[at], dst, t_send.at[q], sem, device(q, y, x, core)), (lhat.at[at], dst, sem)

    for straight, when in ((True, stays), (False, moves)):

        @pl.when(when)
        def _():
            @pl.when(x == z)
            def _():
                _, (src, dst, sem) = t_copy(x, straight)
                pltpu.make_async_copy(src, dst, sem).start()

            def send(q):
                @pl.when(jnp.logical_or(q != x, x != z))
                def _():
                    t_copy(q, straight)[0].start()

            each(4, send)

    swap = remote(tile_hbm, tile.at[core], core_sem.at[0], core_sem.at[1], other_core)
    swap.start()

    def quarter_of(d, e, q):
        return mirrored.at[d, e, span(q * quarter, quarter)]

    def eighth_of(d, e, q, side):
        return mirrored.at[d, e, span(q * quarter + side * eighth, eighth)]

    def lane(nf):
        return jnp.where(nf == 0, y_hi, 1 - y_hi)

    def side_x(side):
        return (x + 1 + 2 * side) % 4

    def from_x(side):
        return (x + 3 + 2 * side) % 4

    def swap_copy(d):
        return remote(stage.at[d], quarter_of(d, y_hi, x), sw_send.at[d], in_recv.at[d, y_hi], swapped)

    def y_copy(d):
        mine = quarter_of(d, y_lo, x)
        return remote(mine, mine, ye_send.at[d], in_recv.at[d, y_lo], y_pair)

    def x_copy(d, nf, side):
        mine = quarter_of(d, lane(nf), x)
        to = device(side_x(side), y, z, core)
        return remote(mine, mine, x_send.at[d, nf, side], x_recv.at[d, nf, side], to)

    def f_copy(d, nf, side):
        relayed = eighth_of(d, lane(nf), from_x(side), side)
        to = device(side_x(side), y, z, core)
        return remote(relayed, relayed, f_send.at[d, nf, side], f_recv.at[d, nf, side], to)

    def arrival(ref, sem):
        return remote(ref, ref, core_sem.at[0], sem, y_far)

    def wide(d, nf):
        return jnp.logical_and(d == 0, jnp.logical_xor(stays, nf == 0))

    def narrow(d, nf):
        return jnp.logical_not(wide(d, nf))

    def pass_copy(j):
        q = pick(j, (from_x(0), from_x(1), (x + 2) % 4))
        ref = quarter_of(0, y_lo, q)
        return remote(ref, ref, p_send.at[j], p_recv.at[j], y_pair)

    def enter(index):
        d, nf = chunk(index)
        e = lane(nf)

        @pl.when(jnp.logical_and(narrow(d, nf), jnp.logical_or(moves, nf == 1)))
        def _():
            arrival(quarter_of(d, e, x), in_recv.at[d, e]).wait_recv()

        @pl.when(jnp.logical_and(moves, nf == 1))
        def _():
            y_copy(d).start()

        @pl.when(narrow(d, nf))
        def _():
            for side in range(2):
                x_copy(d, nf, side).start()

    def relay(index):
        d, nf = chunk(index)

        @pl.when(narrow(d, nf))
        def _():
            for side in range(2):
                arrival(quarter_of(d, lane(nf), from_x(side)), x_recv.at[d, nf, side]).wait_recv()
                f_copy(d, nf, side).start()

                @pl.when(d == 0)
                def _():
                    pass_copy(side).start()

    def complete(d, nf):
        e = lane(nf)

        @pl.when(narrow(d, nf))
        def _():
            for side in range(2):
                arrival(eighth_of(d, e, (x + 2) % 4, side), f_recv.at[d, nf, side]).wait_recv()

            @pl.when(d == 0)
            def _():
                pass_copy(2).start()

        @pl.when(wide(d, nf))
        def _():
            arrival(quarter_of(0, e, x), in_recv.at[0, e]).wait_recv()
            for j, q in enumerate((from_x(0), from_x(1), (x + 2) % 4)):
                arrival(quarter_of(0, e, q), p_recv.at[j]).wait_recv()

    def z_copy(d, nf, h):
        at = span(h * half, half)
        down = jnp.logical_or(d == 1, jnp.logical_and(d == 2, h == 0))
        to = device(x, y, (z + jnp.where(down, 3, 1)) % 4, core)
        return remote(part.at[d, nf, at], heard.at[d - 1, nf, at], z_send.at[d, nf, h], z_recv.at[d - 1, nf, h], to)

    def z_arrival(d, nf, h):
        arrival(heard.at[d - 1, nf, span(h * half, half)], z_recv.at[d - 1, nf, h]).wait_recv()

    def y_reduce(h):
        at = span(h * half, half)
        return remote(y_send.at[at], y_recv.at[at], yr_send.at[h], yr_recv.at[h], y_far)

    def send_far(j):
        h = 1 - j
        z_arrival(1, 1, h)
        z_arrival(3, 1, h)

        def add(i):
            at = span(h * half + i * BLOCK, BLOCK)
            far = part[0, 1, at, :].astype(F32) + (heard[0, 1, at, :].astype(F32) + heard[2, 1, at, :].astype(F32))
            y_send[at, :] = far.astype(BF16)

        each(half // BLOCK, add)
        y_reduce(h).start()

    def add_heard(index):
        d, nf = chunk(index)
        h = jnp.where(d == 1, 0, 1)
        z_arrival(2, nf, h)

        def add(i):
            at = span(h * half + i * BLOCK, BLOCK)
            part[d, nf, at, :] = (part[d, nf, at, :].astype(F32) + heard[1, nf, at, :].astype(F32)).astype(BF16)

        each(half // BLOCK, add)
        z_copy(d, nf, h).start()

    @pl.when(moves)
    def _():
        def move(i):
            d = pick(i, (2, 1, 3, 0))
            arrival(stage.at[d], t_recv.at[d]).wait_recv()
            swap_copy(d).start()

        each(4, move)

    @pl.when(stays)
    def _():
        def pass_on(i):
            d = pick(i, (2, 1, 3, 0))
            arrival(quarter_of(d, y_hi, x), in_recv.at[d, y_hi]).wait_recv()
            y_copy(d).start()

        each(4, pass_on)

    enter(0)
    relay(0)
    for index in range(1, AHEAD):
        enter(index)

    def half_chunk(t):
        i, first = t // 2, t % 2 == 0
        d, nf = chunk(i)
        h = jnp.where(jnp.logical_and(d == 3, nf == 1), t % 2, 1 - t % 2)

        @pl.when(jnp.logical_and(first, i < 7))
        def _():
            relay(i + 1)

        @pl.when(t == 2 * Y_AT)
        def _():
            each(2, send_far)

        @pl.when(jnp.logical_and(first, i < 8 - AHEAD))
        def _():
            enter(i + AHEAD)

        @pl.when(first)
        def _():
            complete(d, nf)

        @pl.when(t == 0)
        def _():
            loads[3].wait()
            swap.wait_recv()

        e = lane(nf)

        def product(j):
            at = span(h * half + j * STEP, STEP)
            acc = jnp.dot(tile[0, at, :], mirrored[d, e, 0:half, :], preferred_element_type=F32)
            acc += jnp.dot(tile[1, at, :], mirrored[d, e, half:, :], preferred_element_type=F32)
            part[d, nf, at, :] = acc.astype(BF16)

        each(half // STEP, product)

        @pl.when(jnp.logical_or(d == 2, d == jnp.where(h == 1, 1, 3)))
        def _():
            z_copy(d, nf, h).start()

        added = choose(t, [[table.get(k, -1) for k in range(16)] for table in ADDED])

        @pl.when(added >= 0)
        def _():
            add_heard(added)

    each(16, half_chunk)
    if Y_AT == 8:
        each(2, send_far)

    total = None
    for h in (1, 0):
        arrival(y_recv.at[span(h * half, half)], yr_recv.at[h]).wait_recv()
        z_arrival(1, 0, h)
        z_arrival(3, 0, h)

        def finish(b):
            at = span((b + h * (blocks // 2)) * BLOCK, BLOCK)
            value = part[0, 0, at, :].astype(F32) + y_recv[at, :].astype(F32)
            value = (value + (heard[0, 0, at, :].astype(F32) + heard[2, 0, at, :].astype(F32))).T
            mask = listed[col, row * blocks + b + h * (blocks // 2)].astype(F32)
            out[:, at] = -(value * mask)
            high = value.astype(BF16)
            split[0:BLOCK, at] = high
            split[BLOCK:, at] = (value - high.astype(F32)).astype(BF16)

        each(blocks // 2, finish)
        both = jnp.dot(split[:, h * half:(h + 1) * half], lhat[h * half:(h + 1) * half, :], preferred_element_type=F32)
        both = both[0:BLOCK] + both[BLOCK:]
        total = both if total is None else total + both

    d_send[...] = total.astype(BF16)

    def d_copy(step):
        to = (row + step + 1) % 8
        return remote(d_send, d_recv.at[row], dg_send.at[step], dg_recv.at[step], (to, col))

    each(7, lambda step: d_copy(step).start())
    d_recv[row] = d_send[...]
    each(7, lambda step: arrival(d_recv.at[(row + 7 - step) % 8], dg_recv.at[step]).wait_recv())
    total = d_recv[0].astype(F32)
    for other in range(1, 8):
        total = total + d_recv[other].astype(F32)
    loads[4].wait()
    diag_out[0] = pivot[0] + total

    swap.wait_send()
    for straight, when in ((True, stays), (False, moves)):

        @pl.when(when)
        def _():
            def sent(q):
                @pl.when(jnp.logical_or(q != x, x != z))
                def _():
                    t_copy(q, straight)[0].wait_send()

            each(4, sent)

    def sent(d):
        @pl.when(moves)
        def _():
            swap_copy(d).wait_send()

        y_copy(d).wait_send()

        def sides(j):
            nf, side = j // 2, j % 2

            @pl.when(narrow(d, nf))
            def _():
                x_copy(d, nf, side).wait_send()
                f_copy(d, nf, side).wait_send()

            @pl.when(d != 0)
            def _():
                z_copy(d, nf, side).wait_send()

        each(4, sides)

    each(4, sent)
    each(3, lambda j: pass_copy(j).wait_send())
    each(2, lambda h: y_reduce(h).wait_send())
    each(7, lambda step: d_copy(step).wait_send())


def per_device(l_panel, inverse_tile, unit_inverse, pivot_inverse, listed):
    rows, width = l_panel.shape
    columns = inverse_tile.shape[1]
    dma = pltpu.SemaphoreType.DMA
    vmem = pl.BlockSpec(memory_space=pltpu.VMEM)
    hbm = pl.BlockSpec(memory_space=pltpu.HBM)
    operands = (listed, l_panel, inverse_tile, unit_inverse, pivot_inverse)
    return pl.pallas_call(
        kernel,
        out_shape=(
            jax.ShapeDtypeStruct((width, rows), F32),
            jax.ShapeDtypeStruct((1, width, width), F32),
        ),
        in_specs=[hbm] * 5,
        out_specs=(vmem, vmem),
        scratch_shapes=[
            pltpu.SMEM(listed.shape, jnp.int32),
            pltpu.VMEM((1, width, width), BF16),
            pltpu.VMEM((1, width, width), F32),
            pltpu.VMEM((rows, width), BF16),
            pltpu.VMEM((rows, width), BF16),
            pltpu.VMEM((2, rows, columns), BF16),
            pltpu.VMEM((4, 2, rows, width), BF16),
            pltpu.VMEM((4, 2, rows, width), BF16),
            pltpu.VMEM((3, 2, rows, width), BF16),
            pltpu.VMEM((rows, width), BF16),
            pltpu.VMEM((rows, width), BF16),
            pltpu.VMEM((4, rows // 4, width), BF16),
            pltpu.VMEM((2 * width, rows), BF16),
            pltpu.VMEM((width, width), BF16),
            pltpu.VMEM((8, width, width), BF16),
            dma((5,)),
            dma((2,)),
            dma((4,)),
            dma((4,)),
            dma((4, 2)),
            dma((4,)),
            dma((4,)),
            dma((4, 2, 2)),
            dma((4, 2, 2)),
            dma((4, 2, 2)),
            dma((4, 2, 2)),
            dma((4, 2, 2)),
            dma((3, 2, 2)),
            dma((3,)),
            dma((3,)),
            dma((2,)),
            dma((2,)),
            dma((7,)),
            dma((7,)),
        ],
        compiler_params=pltpu.CompilerParams(
            collective_id=0, has_side_effects=True, vmem_limit_bytes=36 << 20
        ),
    )(*(pltpu.with_memory_space_constraint(a, pltpu.HBM) for a in operands))


def solution(mesh):
    return jax.shard_map(
        per_device,
        mesh=mesh,
        in_specs=(
            P("prow", "pcol"),
            P("prow", "pcol"),
            P("pcol", None, None),
            P("pcol", None, None),
            P(),
        ),
        out_specs=(P("pcol", "prow"), P("pcol", None, None)),
        check_vma=False,
    )
```

```python
import jax
import jax.numpy as jnp
from jax import lax
from jax.experimental import pallas as pl
from jax.experimental.pallas import tpu as pltpu
from jax.sharding import PartitionSpec as P

MESH = pl.DeviceIdType.MESH
BLOCK = 128
STEP = 1024
ORDER = (
    ((2, 0), (2, 1), (1, 1), (3, 1), (0, 0), (0, 1), (1, 0), (3, 0)),
    ((2, 1), (2, 0), (1, 1), (3, 1), (0, 1), (0, 0), (1, 0), (3, 0)),
)
ADDED = ({7: 2, 9: 3, 13: 6, 14: 7}, {7: 2, 9: 3, 13: 6, 14: 7})
Y_AT = 7
AHEAD = 4
F32 = jnp.float32
BF16 = jnp.bfloat16


def device(x, y, z, core):
    return ((y % 2) * 4 + x, (y // 2) * 8 + z * 2 + core)


def pick(index, table):
    value = table[-1]
    for at in range(len(table) - 2, -1, -1):
        value = jnp.where(index == at, table[at], value)
    return value


def kernel(
    listed_hbm, panel_hbm, tile_hbm, unit_hbm, pivot_hbm, out, diag_out,
    listed, unit, pivot, panel, lhat, tile, mirrored, part, heard, y_send, y_recv,
    stage, split, d_send, d_recv,
    local_sem, core_sem, t_send, t_recv, in_recv, sw_send, ye_send,
    x_send, x_recv, f_send, f_recv, z_send, z_recv, p_send, p_recv, yr_send, yr_recv, dg_send, dg_recv,
):
    row, col = lax.axis_index("prow"), lax.axis_index("pcol")
    x, y_lo = row % 4, row // 4
    y_hi, z, core = col // 8, (col // 2) % 4, col % 2
    y = 2 * y_hi + y_lo
    y_swap = 2 * y_lo + y_hi
    y_other = 2 * y_hi + 1 - y_lo
    stays = y_lo == y_hi
    moves = y_lo != y_hi

    def choose(index, tables):
        return jnp.where(stays, pick(index, tables[0]), pick(index, tables[1]))

    def chunk(index):
        return tuple(choose(index, [[c[k] for c in order] for order in ORDER]) for k in range(2))

    rows = panel.shape[0]
    half, quarter, eighth = rows // 2, rows // 4, rows // 8
    blocks = rows // BLOCK

    loads = [
        pltpu.make_async_copy(src, dst, local_sem.at[i])
        for i, (src, dst) in enumerate(
            (
                (panel_hbm, panel),
                (listed_hbm, listed),
                (unit_hbm, unit),
                (tile_hbm, tile.at[core]),
                (pivot_hbm, pivot),
            )
        )
    ]
    for load in loads:
        load.start()

    def remote(src, dst, send, recv, to):
        return pltpu.make_async_remote_copy(
            src_ref=src, dst_ref=dst, send_sem=send, recv_sem=recv, device_id=to, device_id_type=MESH
        )

    def each(count, body):
        def step(i, carry):
            body(i)
            return carry

        lax.fori_loop(0, count, step, 0)

    def span(start, size):
        return pl.ds(pl.multiple_of(start, size), size)

    barrier = pltpu.get_barrier_semaphore()

    def greet(to):
        pl.semaphore_signal(barrier, inc=1, device_id=to, device_id_type=MESH)

    y_pair = device(x, y_other, z, core)
    y_far = device(x, 2 * (1 - y_hi) + y_lo, z, core)
    other_core = device(x, y, z, 1 - core)
    swapped = device(x, y_swap, z, core)
    for step in range(1, 8):
        greet(((row + step) % 8, col))
    for to in (device(x, y, (z + 1) % 4, core), device(x, y, (z + 3) % 4, core), y_far, other_core, swapped):
        greet(to)

    def greet_group(q):
        greet(device(q, y, x, core))
        greet(device(z, y, q, core))

    each(4, greet_group)

    for load in loads[:3]:
        load.wait()

    def lhat_block(b):
        at = span(b * BLOCK, BLOCK)
        mask = listed[col, row * blocks + b].astype(F32)
        masked = (panel[at, :].astype(F32) * mask).astype(BF16)
        lhat[at, :] = jnp.dot(masked, unit[0], preferred_element_type=F32).astype(BF16)

    each(blocks, lhat_block)
    pl.semaphore_wait(barrier, 20)

    d_mine = (x + 4 - z) % 4

    def t_copy(q, straight):
        at = span(q * quarter, quarter)
        if straight:
            dst, sem = mirrored.at[d_mine, y_hi, at], in_recv.at[d_mine, y_hi]
        else:
            dst, sem = stage.at[d_mine], t_recv.at[d_mine]
        return remote(lhat.at[at], dst, t_send.at[q], sem, device(q, y, x, core)), (lhat.at[at], dst, sem)

    for straight, when in ((True, stays), (False, moves)):

        @pl.when(when)
        def _():
            @pl.when(x == z)
            def _():
                _, (src, dst, sem) = t_copy(x, straight)
                pltpu.make_async_copy(src, dst, sem).start()

            def send(q):
                @pl.when(jnp.logical_or(q != x, x != z))
                def _():
                    t_copy(q, straight)[0].start()

            each(4, send)

    swap = remote(tile_hbm, tile.at[core], core_sem.at[0], core_sem.at[1], other_core)
    swap.start()

    def quarter_of(d, e, q):
        return mirrored.at[d, e, span(q * quarter, quarter)]

    def eighth_of(d, e, q, side):
        return mirrored.at[d, e, span(q * quarter + side * eighth, eighth)]

    def lane(nf):
        return jnp.where(nf == 0, y_hi, 1 - y_hi)

    def side_x(side):
        return (x + 1 + 2 * side) % 4

    def from_x(side):
        return (x + 3 + 2 * side) % 4

    def swap_copy(d):
        return remote(stage.at[d], quarter_of(d, y_hi, x), sw_send.at[d], in_recv.at[d, y_hi], swapped)

    def y_copy(d):
        mine = quarter_of(d, y_lo, x)
        return remote(mine, mine, ye_send.at[d], in_recv.at[d, y_lo], y_pair)

    def x_copy(d, nf, side):
        mine = quarter_of(d, lane(nf), x)
        to = device(side_x(side), y, z, core)
        return remote(mine, mine, x_send.at[d, nf, side], x_recv.at[d, nf, side], to)

    def f_copy(d, nf, side):
        relayed = eighth_of(d, lane(nf), from_x(side), side)
        to = device(side_x(side), y, z, core)
        return remote(relayed, relayed, f_send.at[d, nf, side], f_recv.at[d, nf, side], to)

    def arrival(ref, sem):
        return remote(ref, ref, core_sem.at[0], sem, y_far)

    def wide(d, nf):
        return jnp.logical_and(d == 0, jnp.logical_xor(stays, nf == 0))

    def narrow(d, nf):
        return jnp.logical_not(wide(d, nf))

    def pass_copy(j):
        q = pick(j, (from_x(0), from_x(1), (x + 2) % 4))
        ref = quarter_of(0, y_lo, q)
        return remote(ref, ref, p_send.at[j], p_recv.at[j], y_pair)

    def enter(index):
        d, nf = chunk(index)
        e = lane(nf)

        @pl.when(jnp.logical_and(narrow(d, nf), jnp.logical_or(moves, nf == 1)))
        def _():
            arrival(quarter_of(d, e, x), in_recv.at[d, e]).wait_recv()

        @pl.when(jnp.logical_and(moves, nf == 1))
        def _():
            y_copy(d).start()

        @pl.when(narrow(d, nf))
        def _():
            for side in range(2):
                x_copy(d, nf, side).start()

    def relay(index):
        d, nf = chunk(index)

        @pl.when(narrow(d, nf))
        def _():
            for side in range(2):
                arrival(quarter_of(d, lane(nf), from_x(side)), x_recv.at[d, nf, side]).wait_recv()
                f_copy(d, nf, side).start()

                @pl.when(d == 0)
                def _():
                    pass_copy(side).start()

    def complete(d, nf):
        e = lane(nf)

        @pl.when(narrow(d, nf))
        def _():
            for side in range(2):
                arrival(eighth_of(d, e, (x + 2) % 4, side), f_recv.at[d, nf, side]).wait_recv()

            @pl.when(d == 0)
            def _():
                pass_copy(2).start()

        @pl.when(wide(d, nf))
        def _():
            arrival(quarter_of(0, e, x), in_recv.at[0, e]).wait_recv()
            for j, q in enumerate((from_x(0), from_x(1), (x + 2) % 4)):
                arrival(quarter_of(0, e, q), p_recv.at[j]).wait_recv()

    def z_copy(d, nf, h):
        at = span(h * half, half)
        down = jnp.logical_or(d == 1, jnp.logical_and(d == 2, h == 0))
        to = device(x, y, (z + jnp.where(down, 3, 1)) % 4, core)
        return remote(part.at[d, nf, at], heard.at[d - 1, nf, at], z_send.at[d, nf, h], z_recv.at[d - 1, nf, h], to)

    def z_arrival(d, nf, h):
        arrival(heard.at[d - 1, nf, span(h * half, half)], z_recv.at[d - 1, nf, h]).wait_recv()

    def y_reduce(h):
        at = span(h * half, half)
        return remote(y_send.at[at], y_recv.at[at], yr_send.at[h], yr_recv.at[h], y_far)

    def send_far(j):
        h = 1 - j
        z_arrival(1, 1, h)
        z_arrival(3, 1, h)

        def add(i):
            at = span(h * half + i * 2 * BLOCK, 2 * BLOCK)
            far = part[0, 1, at, :].astype(F32) + (heard[0, 1, at, :].astype(F32) + heard[2, 1, at, :].astype(F32))
            y_send[at, :] = far.astype(BF16)

        each(half // (2 * BLOCK), add)
        y_reduce(h).start()

    def add_heard(index):
        d, nf = chunk(index)
        h = jnp.where(d == 1, 0, 1)
        z_arrival(2, nf, h)

        def add(i):
            at = span(h * half + i * 2 * BLOCK, 2 * BLOCK)
            part[d, nf, at, :] = (part[d, nf, at, :].astype(F32) + heard[1, nf, at, :].astype(F32)).astype(BF16)

        each(half // (2 * BLOCK), add)
        z_copy(d, nf, h).start()

    @pl.when(moves)
    def _():
        def move(i):
            d = pick(i, (2, 1, 3, 0))
            arrival(stage.at[d], t_recv.at[d]).wait_recv()
            swap_copy(d).start()

        each(4, move)

    @pl.when(stays)
    def _():
        def pass_on(i):
            d = pick(i, (2, 1, 3, 0))
            arrival(quarter_of(d, y_hi, x), in_recv.at[d, y_hi]).wait_recv()
            y_copy(d).start()

        each(4, pass_on)

    enter(0)
    relay(0)
    for index in range(1, AHEAD):
        enter(index)

    def half_chunk(t):
        i, first = t // 2, t % 2 == 0
        d, nf = chunk(i)
        h = jnp.where(jnp.logical_and(d == 3, nf == 1), t % 2, 1 - t % 2)

        @pl.when(jnp.logical_and(first, i < 7))
        def _():
            relay(i + 1)

        @pl.when(t == 2 * Y_AT)
        def _():
            each(2, send_far)

        @pl.when(jnp.logical_and(first, i < 8 - AHEAD))
        def _():
            enter(i + AHEAD)

        @pl.when(first)
        def _():
            complete(d, nf)

        @pl.when(t == 0)
        def _():
            loads[3].wait()
            swap.wait_recv()

        e = lane(nf)

        def product(j):
            at = span(h * half + j * STEP, STEP)
            acc = jnp.dot(tile[0, at, :], mirrored[d, e, 0:half, :], preferred_element_type=F32)
            acc += jnp.dot(tile[1, at, :], mirrored[d, e, half:, :], preferred_element_type=F32)
            part[d, nf, at, :] = acc.astype(BF16)

        each(half // STEP, product)

        @pl.when(jnp.logical_or(d == 2, d == jnp.where(h == 1, 1, 3)))
        def _():
            z_copy(d, nf, h).start()

        added = choose(t, [[table.get(k, -1) for k in range(16)] for table in ADDED])

        @pl.when(added >= 0)
        def _():
            add_heard(added)

    each(16, half_chunk)
    if Y_AT == 8:
        each(2, send_far)

    total = None
    for h in (1, 0):
        arrival(y_recv.at[span(h * half, half)], yr_recv.at[h]).wait_recv()
        z_arrival(1, 0, h)
        z_arrival(3, 0, h)

        def finish(group):
            for step in range(4):
                b = 4 * group + step + h * (blocks // 2)
                at = span(b * BLOCK, BLOCK)
                value = part[0, 0, at, :].astype(F32) + y_recv[at, :].astype(F32)
                value = (value + (heard[0, 0, at, :].astype(F32) + heard[2, 0, at, :].astype(F32))).T
                mask = listed[col, row * blocks + b].astype(F32)
                out[:, at] = -(value * mask)
                high = value.astype(BF16)
                split[0:BLOCK, at] = high
                split[BLOCK:, at] = (value - high.astype(F32)).astype(BF16)

        each(blocks // 8, finish)
        both = jnp.dot(split[:, h * half:(h + 1) * half], lhat[h * half:(h + 1) * half, :], preferred_element_type=F32)
        both = both[0:BLOCK] + both[BLOCK:]
        total = both if total is None else total + both

    d_send[...] = total.astype(BF16)

    def d_copy(step):
        to = (row + step + 1) % 8
        return remote(d_send, d_recv.at[row], dg_send.at[step], dg_recv.at[step], (to, col))

    each(7, lambda step: d_copy(step).start())
    d_recv[row] = d_send[...]
    swap.wait_send()
    for straight, when in ((True, stays), (False, moves)):

        @pl.when(when)
        def _():
            def sent(q):
                @pl.when(jnp.logical_or(q != x, x != z))
                def _():
                    t_copy(q, straight)[0].wait_send()

            each(4, sent)

    def sent(d):
        @pl.when(moves)
        def _():
            swap_copy(d).wait_send()

        y_copy(d).wait_send()

        def sides(j):
            nf, side = j // 2, j % 2

            @pl.when(narrow(d, nf))
            def _():
                x_copy(d, nf, side).wait_send()
                f_copy(d, nf, side).wait_send()

            @pl.when(d != 0)
            def _():
                z_copy(d, nf, side).wait_send()

        each(4, sides)

    each(4, sent)
    each(3, lambda j: pass_copy(j).wait_send())
    each(2, lambda h: y_reduce(h).wait_send())
    each(7, lambda step: arrival(d_recv.at[(row + 7 - step) % 8], dg_recv.at[step]).wait_recv())
    total = d_recv[0].astype(F32)
    for other in range(1, 8):
        total = total + d_recv[other].astype(F32)
    loads[4].wait()
    diag_out[0] = pivot[0] + total

    each(7, lambda step: d_copy(step).wait_send())


def per_device(l_panel, inverse_tile, unit_inverse, pivot_inverse, listed):
    rows, width = l_panel.shape
    columns = inverse_tile.shape[1]
    dma = pltpu.SemaphoreType.DMA
    vmem = pl.BlockSpec(memory_space=pltpu.VMEM)
    hbm = pl.BlockSpec(memory_space=pltpu.HBM)
    operands = (listed, l_panel, inverse_tile, unit_inverse, pivot_inverse)
    return pl.pallas_call(
        kernel,
        out_shape=(
            jax.ShapeDtypeStruct((width, rows), F32),
            jax.ShapeDtypeStruct((1, width, width), F32),
        ),
        in_specs=[hbm] * 5,
        out_specs=(vmem, vmem),
        scratch_shapes=[
            pltpu.SMEM(listed.shape, jnp.int32),
            pltpu.VMEM((1, width, width), BF16),
            pltpu.VMEM((1, width, width), F32),
            pltpu.VMEM((rows, width), BF16),
            pltpu.VMEM((rows, width), BF16),
            pltpu.VMEM((2, rows, columns), BF16),
            pltpu.VMEM((4, 2, rows, width), BF16),
            pltpu.VMEM((4, 2, rows, width), BF16),
            pltpu.VMEM((3, 2, rows, width), BF16),
            pltpu.VMEM((rows, width), BF16),
            pltpu.VMEM((rows, width), BF16),
            pltpu.VMEM((4, rows // 4, width), BF16),
            pltpu.VMEM((2 * width, rows), BF16),
            pltpu.VMEM((width, width), BF16),
            pltpu.VMEM((8, width, width), BF16),
            dma((5,)),
            dma((2,)),
            dma((4,)),
            dma((4,)),
            dma((4, 2)),
            dma((4,)),
            dma((4,)),
            dma((4, 2, 2)),
            dma((4, 2, 2)),
            dma((4, 2, 2)),
            dma((4, 2, 2)),
            dma((4, 2, 2)),
            dma((3, 2, 2)),
            dma((3,)),
            dma((3,)),
            dma((2,)),
            dma((2,)),
            dma((7,)),
            dma((7,)),
        ],
        compiler_params=pltpu.CompilerParams(
            collective_id=0, has_side_effects=True, vmem_limit_bytes=36 << 20
        ),
    )(*(pltpu.with_memory_space_constraint(a, pltpu.HBM) for a in operands))


def solution(mesh):
    return jax.shard_map(
        per_device,
        mesh=mesh,
        in_specs=(
            P("prow", "pcol"),
            P("prow", "pcol"),
            P("pcol", None, None),
            P("pcol", None, None),
            P(),
        ),
        out_specs=(P("pcol", "prow"), P("pcol", None, None)),
        check_vma=False,
    )
```

```python
import jax
import jax.numpy as jnp
from jax import lax
from jax.experimental import pallas as pl
from jax.experimental.pallas import tpu as pltpu
from jax.sharding import PartitionSpec as P

MESH = pl.DeviceIdType.MESH
BLOCK = 128
STEP = 1024
ORDER = (
    ((2, 0), (2, 1), (1, 1), (3, 1), (0, 0), (0, 1), (1, 0), (3, 0)),
    ((2, 1), (2, 0), (1, 1), (3, 1), (0, 1), (0, 0), (1, 0), (3, 0)),
)
ADDED = ({7: 2, 9: 3, 13: 6, 14: 7}, {7: 2, 9: 3, 13: 6, 14: 7})
Y_AT = 7
AHEAD = 4
F32 = jnp.float32
BF16 = jnp.bfloat16


def device(x, y, z, core):
    return ((y % 2) * 4 + x, (y // 2) * 8 + z * 2 + core)


def pick(index, table):
    value = table[-1]
    for at in range(len(table) - 2, -1, -1):
        value = jnp.where(index == at, table[at], value)
    return value


def kernel(
    listed_hbm, panel_hbm, tile_hbm, unit_hbm, pivot_hbm, out, diag_out,
    listed, unit, pivot, panel, lhat, tile, mirrored, part, heard, y_send, y_recv,
    stage, split, d_send, d_recv,
    local_sem, core_sem, t_send, t_recv, in_recv, sw_send, ye_send,
    x_send, x_recv, f_send, f_recv, z_send, z_recv, p_send, p_recv, yr_send, yr_recv, dg_send, dg_recv,
):
    row, col = lax.axis_index("prow"), lax.axis_index("pcol")
    x, y_lo = row % 4, row // 4
    y_hi, z, core = col // 8, (col // 2) % 4, col % 2
    y = 2 * y_hi + y_lo
    y_swap = 2 * y_lo + y_hi
    y_other = 2 * y_hi + 1 - y_lo
    stays = y_lo == y_hi
    moves = y_lo != y_hi

    def choose(index, tables):
        return jnp.where(stays, pick(index, tables[0]), pick(index, tables[1]))

    def chunk(index):
        return tuple(choose(index, [[c[k] for c in order] for order in ORDER]) for k in range(2))

    rows = panel.shape[0]
    half, quarter, eighth = rows // 2, rows // 4, rows // 8
    blocks = rows // BLOCK

    loads = [
        pltpu.make_async_copy(src, dst, local_sem.at[i])
        for i, (src, dst) in enumerate(
            (
                (panel_hbm, panel),
                (listed_hbm, listed),
                (unit_hbm, unit),
                (tile_hbm, tile.at[core]),
                (pivot_hbm, pivot),
            )
        )
    ]
    for load in loads:
        load.start()

    def remote(src, dst, send, recv, to):
        return pltpu.make_async_remote_copy(
            src_ref=src, dst_ref=dst, send_sem=send, recv_sem=recv, device_id=to, device_id_type=MESH
        )

    def each(count, body):
        def step(i, carry):
            body(i)
            return carry

        lax.fori_loop(0, count, step, 0)

    def span(start, size):
        return pl.ds(pl.multiple_of(start, size), size)

    barrier = pltpu.get_barrier_semaphore()

    def greet(to):
        pl.semaphore_signal(barrier, inc=1, device_id=to, device_id_type=MESH)

    y_pair = device(x, y_other, z, core)
    y_far = device(x, 2 * (1 - y_hi) + y_lo, z, core)
    other_core = device(x, y, z, 1 - core)
    swapped = device(x, y_swap, z, core)
    for step in range(1, 8):
        greet(((row + step) % 8, col))
    for to in (device(x, y, (z + 1) % 4, core), device(x, y, (z + 3) % 4, core), y_far, other_core, swapped):
        greet(to)

    def greet_group(q):
        greet(device(q, y, x, core))
        greet(device(z, y, q, core))

    each(4, greet_group)

    for load in loads[:3]:
        load.wait()

    def lhat_quarter(q):
        parts = []
        for b in range(quarter // BLOCK):
            mask = listed[col, row * blocks + q * (quarter // BLOCK) + b].astype(F32)
            parts.append((panel[span(q * quarter + b * BLOCK, BLOCK), :].astype(F32) * mask).astype(BF16))
        normalized = jnp.dot(jnp.concatenate(parts, axis=0), unit[0], preferred_element_type=F32)
        lhat[span(q * quarter, quarter), :] = normalized.astype(BF16)

    each(4, lhat_quarter)
    pl.semaphore_wait(barrier, 20)

    d_mine = (x + 4 - z) % 4

    def t_copy(q, straight):
        at = span(q * quarter, quarter)
        if straight:
            dst, sem = mirrored.at[d_mine, y_hi, at], in_recv.at[d_mine, y_hi]
        else:
            dst, sem = stage.at[d_mine], t_recv.at[d_mine]
        return remote(lhat.at[at], dst, t_send.at[q], sem, device(q, y, x, core)), (lhat.at[at], dst, sem)

    for straight, when in ((True, stays), (False, moves)):

        @pl.when(when)
        def _():
            @pl.when(x == z)
            def _():
                _, (src, dst, sem) = t_copy(x, straight)
                pltpu.make_async_copy(src, dst, sem).start()

            def send(q):
                @pl.when(jnp.logical_or(q != x, x != z))
                def _():
                    t_copy(q, straight)[0].start()

            each(4, send)

    swap = remote(tile_hbm, tile.at[core], core_sem.at[0], core_sem.at[1], other_core)
    swap.start()

    def quarter_of(d, e, q):
        return mirrored.at[d, e, span(q * quarter, quarter)]

    def eighth_of(d, e, q, side):
        return mirrored.at[d, e, span(q * quarter + side * eighth, eighth)]

    def lane(nf):
        return jnp.where(nf == 0, y_hi, 1 - y_hi)

    def side_x(side):
        return (x + 1 + 2 * side) % 4

    def from_x(side):
        return (x + 3 + 2 * side) % 4

    def swap_copy(d):
        return remote(stage.at[d], quarter_of(d, y_hi, x), sw_send.at[d], in_recv.at[d, y_hi], swapped)

    def y_copy(d):
        mine = quarter_of(d, y_lo, x)
        return remote(mine, mine, ye_send.at[d], in_recv.at[d, y_lo], y_pair)

    def x_copy(d, nf, side):
        mine = quarter_of(d, lane(nf), x)
        to = device(side_x(side), y, z, core)
        return remote(mine, mine, x_send.at[d, nf, side], x_recv.at[d, nf, side], to)

    def f_copy(d, nf, side):
        relayed = eighth_of(d, lane(nf), from_x(side), side)
        to = device(side_x(side), y, z, core)
        return remote(relayed, relayed, f_send.at[d, nf, side], f_recv.at[d, nf, side], to)

    def arrival(ref, sem):
        return remote(ref, ref, core_sem.at[0], sem, y_far)

    def wide(d, nf):
        return jnp.logical_and(d == 0, jnp.logical_xor(stays, nf == 0))

    def narrow(d, nf):
        return jnp.logical_not(wide(d, nf))

    def pass_copy(j):
        q = pick(j, (from_x(0), from_x(1), (x + 2) % 4))
        ref = quarter_of(0, y_lo, q)
        return remote(ref, ref, p_send.at[j], p_recv.at[j], y_pair)

    def enter(index):
        d, nf = chunk(index)
        e = lane(nf)

        @pl.when(jnp.logical_and(narrow(d, nf), jnp.logical_or(moves, nf == 1)))
        def _():
            arrival(quarter_of(d, e, x), in_recv.at[d, e]).wait_recv()

        @pl.when(jnp.logical_and(moves, nf == 1))
        def _():
            y_copy(d).start()

        @pl.when(narrow(d, nf))
        def _():
            for side in range(2):
                x_copy(d, nf, side).start()

    def relay(index):
        d, nf = chunk(index)

        @pl.when(narrow(d, nf))
        def _():
            for side in range(2):
                arrival(quarter_of(d, lane(nf), from_x(side)), x_recv.at[d, nf, side]).wait_recv()
                f_copy(d, nf, side).start()

                @pl.when(d == 0)
                def _():
                    pass_copy(side).start()

    def complete(d, nf):
        e = lane(nf)

        @pl.when(narrow(d, nf))
        def _():
            for side in range(2):
                arrival(eighth_of(d, e, (x + 2) % 4, side), f_recv.at[d, nf, side]).wait_recv()

            @pl.when(d == 0)
            def _():
                pass_copy(2).start()

        @pl.when(wide(d, nf))
        def _():
            arrival(quarter_of(0, e, x), in_recv.at[0, e]).wait_recv()
            for j, q in enumerate((from_x(0), from_x(1), (x + 2) % 4)):
                arrival(quarter_of(0, e, q), p_recv.at[j]).wait_recv()

    def z_copy(d, nf, h):
        at = span(h * half, half)
        down = jnp.logical_or(d == 1, jnp.logical_and(d == 2, h == 0))
        to = device(x, y, (z + jnp.where(down, 3, 1)) % 4, core)
        return remote(part.at[d, nf, at], heard.at[d - 1, nf, at], z_send.at[d, nf, h], z_recv.at[d - 1, nf, h], to)

    def z_arrival(d, nf, h):
        arrival(heard.at[d - 1, nf, span(h * half, half)], z_recv.at[d - 1, nf, h]).wait_recv()

    def y_reduce(h):
        at = span(h * half, half)
        return remote(y_send.at[at], y_recv.at[at], yr_send.at[h], yr_recv.at[h], y_far)

    def send_far(j):
        h = 1 - j
        z_arrival(1, 1, h)
        z_arrival(3, 1, h)

        def add(i):
            at = span(h * half + i * 2 * BLOCK, 2 * BLOCK)
            far = part[0, 1, at, :].astype(F32) + (heard[0, 1, at, :].astype(F32) + heard[2, 1, at, :].astype(F32))
            y_send[at, :] = far.astype(BF16)

        each(half // (2 * BLOCK), add)
        y_reduce(h).start()

    def add_heard(index):
        d, nf = chunk(index)
        h = jnp.where(d == 1, 0, 1)
        z_arrival(2, nf, h)

        def add(i):
            at = span(h * half + i * 2 * BLOCK, 2 * BLOCK)
            part[d, nf, at, :] = (part[d, nf, at, :].astype(F32) + heard[1, nf, at, :].astype(F32)).astype(BF16)

        each(half // (2 * BLOCK), add)
        z_copy(d, nf, h).start()

    @pl.when(moves)
    def _():
        def move(i):
            d = pick(i, (2, 1, 3, 0))
            arrival(stage.at[d], t_recv.at[d]).wait_recv()
            swap_copy(d).start()

        each(4, move)

    @pl.when(stays)
    def _():
        def pass_on(i):
            d = pick(i, (2, 1, 3, 0))
            arrival(quarter_of(d, y_hi, x), in_recv.at[d, y_hi]).wait_recv()
            y_copy(d).start()

        each(4, pass_on)

    enter(0)
    relay(0)
    for index in range(1, AHEAD):
        enter(index)

    def half_chunk(t):
        i, first = t // 2, t % 2 == 0
        d, nf = chunk(i)
        h = jnp.where(jnp.logical_and(d == 3, nf == 1), t % 2, 1 - t % 2)

        @pl.when(jnp.logical_and(first, i < 7))
        def _():
            relay(i + 1)

        @pl.when(t == 2 * Y_AT)
        def _():
            each(2, send_far)

        @pl.when(jnp.logical_and(first, i < 8 - AHEAD))
        def _():
            enter(i + AHEAD)

        @pl.when(first)
        def _():
            complete(d, nf)

        @pl.when(t == 0)
        def _():
            loads[3].wait()
            swap.wait_recv()

        e = lane(nf)

        def product(j):
            at = span(h * half + j * STEP, STEP)
            acc = jnp.dot(tile[0, at, :], mirrored[d, e, 0:half, :], preferred_element_type=F32)
            acc += jnp.dot(tile[1, at, :], mirrored[d, e, half:, :], preferred_element_type=F32)
            part[d, nf, at, :] = acc.astype(BF16)

        each(half // STEP, product)

        @pl.when(jnp.logical_or(d == 2, d == jnp.where(h == 1, 1, 3)))
        def _():
            z_copy(d, nf, h).start()

        added = choose(t, [[table.get(k, -1) for k in range(16)] for table in ADDED])

        @pl.when(added >= 0)
        def _():
            add_heard(added)

    each(16, half_chunk)
    if Y_AT == 8:
        each(2, send_far)

    total = None
    for h in (1, 0):
        arrival(y_recv.at[span(h * half, half)], yr_recv.at[h]).wait_recv()
        z_arrival(1, 0, h)
        z_arrival(3, 0, h)

        def finish(group):
            for step in range(4):
                b = 4 * group + step + h * (blocks // 2)
                at = span(b * BLOCK, BLOCK)
                value = part[0, 0, at, :].astype(F32) + y_recv[at, :].astype(F32)
                value = (value + (heard[0, 0, at, :].astype(F32) + heard[2, 0, at, :].astype(F32))).T
                mask = listed[col, row * blocks + b].astype(F32)
                out[:, at] = -(value * mask)
                high = value.astype(BF16)
                split[0:BLOCK, at] = high
                split[BLOCK:, at] = (value - high.astype(F32)).astype(BF16)

        each(blocks // 8, finish)
        both = jnp.dot(split[:, h * half:(h + 1) * half], lhat[h * half:(h + 1) * half, :], preferred_element_type=F32)
        both = both[0:BLOCK] + both[BLOCK:]
        total = both if total is None else total + both

    d_send[...] = total.astype(BF16)

    def d_copy(step):
        to = (row + step + 1) % 8
        return remote(d_send, d_recv.at[row], dg_send.at[step], dg_recv.at[step], (to, col))

    each(7, lambda step: d_copy(step).start())
    d_recv[row] = d_send[...]
    swap.wait_send()
    for straight, when in ((True, stays), (False, moves)):

        @pl.when(when)
        def _():
            def sent(q):
                @pl.when(jnp.logical_or(q != x, x != z))
                def _():
                    t_copy(q, straight)[0].wait_send()

            each(4, sent)

    def sent(d):
        @pl.when(moves)
        def _():
            swap_copy(d).wait_send()

        y_copy(d).wait_send()

        def sides(j):
            nf, side = j // 2, j % 2

            @pl.when(narrow(d, nf))
            def _():
                x_copy(d, nf, side).wait_send()
                f_copy(d, nf, side).wait_send()

            @pl.when(d != 0)
            def _():
                z_copy(d, nf, side).wait_send()

        each(4, sides)

    each(4, sent)
    each(3, lambda j: pass_copy(j).wait_send())
    each(2, lambda h: y_reduce(h).wait_send())
    each(7, lambda step: arrival(d_recv.at[(row + 7 - step) % 8], dg_recv.at[step]).wait_recv())
    total = d_recv[0].astype(F32)
    for other in range(1, 8):
        total = total + d_recv[other].astype(F32)
    loads[4].wait()
    diag_out[0] = pivot[0] + total

    each(7, lambda step: d_copy(step).wait_send())


def per_device(l_panel, inverse_tile, unit_inverse, pivot_inverse, listed):
    rows, width = l_panel.shape
    columns = inverse_tile.shape[1]
    dma = pltpu.SemaphoreType.DMA
    vmem = pl.BlockSpec(memory_space=pltpu.VMEM)
    hbm = pl.BlockSpec(memory_space=pltpu.HBM)
    operands = (listed, l_panel, inverse_tile, unit_inverse, pivot_inverse)
    return pl.pallas_call(
        kernel,
        out_shape=(
            jax.ShapeDtypeStruct((width, rows), F32),
            jax.ShapeDtypeStruct((1, width, width), F32),
        ),
        in_specs=[hbm] * 5,
        out_specs=(vmem, vmem),
        scratch_shapes=[
            pltpu.SMEM(listed.shape, jnp.int32),
            pltpu.VMEM((1, width, width), BF16),
            pltpu.VMEM((1, width, width), F32),
            pltpu.VMEM((rows, width), BF16),
            pltpu.VMEM((rows, width), BF16),
            pltpu.VMEM((2, rows, columns), BF16),
            pltpu.VMEM((4, 2, rows, width), BF16),
            pltpu.VMEM((4, 2, rows, width), BF16),
            pltpu.VMEM((3, 2, rows, width), BF16),
            pltpu.VMEM((rows, width), BF16),
            pltpu.VMEM((rows, width), BF16),
            pltpu.VMEM((4, rows // 4, width), BF16),
            pltpu.VMEM((2 * width, rows), BF16),
            pltpu.VMEM((width, width), BF16),
            pltpu.VMEM((8, width, width), BF16),
            dma((5,)),
            dma((2,)),
            dma((4,)),
            dma((4,)),
            dma((4, 2)),
            dma((4,)),
            dma((4,)),
            dma((4, 2, 2)),
            dma((4, 2, 2)),
            dma((4, 2, 2)),
            dma((4, 2, 2)),
            dma((4, 2, 2)),
            dma((3, 2, 2)),
            dma((3,)),
            dma((3,)),
            dma((2,)),
            dma((2,)),
            dma((7,)),
            dma((7,)),
        ],
        compiler_params=pltpu.CompilerParams(
            collective_id=0, has_side_effects=True, vmem_limit_bytes=36 << 20
        ),
    )(*(pltpu.with_memory_space_constraint(a, pltpu.HBM) for a in operands))


def solution(mesh):
    return jax.shard_map(
        per_device,
        mesh=mesh,
        in_specs=(
            P("prow", "pcol"),
            P("prow", "pcol"),
            P("pcol", None, None),
            P("pcol", None, None),
            P(),
        ),
        out_specs=(P("pcol", "prow"), P("pcol", None, None)),
        check_vma=False,
    )
```
